32 devices in a mesh: tm: 2 (over x), diamond: 2 (over y), tile: 8 (over z, core).
Axes of the slice: x: 2, y: 2, z: 4, core: 2. Of those that a mesh axis runs over, the one named last changes fastest.
Arguments:
- activations: bfloat16 [8, 2, 32, 64, 256], P('tm', 'diamond', 'tile'), may hold values from -6 to 6
- upstream: bfloat16 [8, 2, 32, 64, 256], P('tm', 'diamond', 'tile'), may hold values from -16 to 16
- hex_weight: bfloat16 [7, 64, 64], replicated, may hold values from -0.25 to 0.25
- time_weight: bfloat16 [3, 64, 64], replicated, may hold values from -0.4375 to 0.4375
- left_map: int32 [2, 32], replicated, may hold values from 0 to 31, each once within a row
- right_map: int32 [2, 32], replicated, may hold values from 0 to 31, each once within a row
Outputs:
- grad_input: bfloat16 [8, 2, 32, 64, 256], P('tm', 'diamond', 'tile')
- grad_hex: float32 [7, 64, 64], replicated
- grad_time: float32 [3, 64, 64], replicated
The draws below stay inside these ranges and needn't reach their ends.
Inputs may be any that keep to these rules, and one draw needn't show every extreme that they name: Each row of left_map holds every number of 0 to 31 once. Each row of right_map holds every number of 0 to 31 once.
All inputs are finite; a program needn't handle non-finite values.
Results may differ from the reference program's by a relative error of at most 0.0035.
Values may be sent and summed in bfloat16 or wider, within the bound.
A program may use at most 64 MiB of HBM per device.

```python
import jax
import jax.numpy as jnp
from jax import lax

CH = 64
COLS = 256
FRAMES = 8
CHARTS = 2
ROWS = 32


def draw_upstream(key, part):
    noise_key = jax.random.fold_in(key, 0)
    shape = (FRAMES, CHARTS, ROWS, CH, COLS)
    chart = jnp.arange(CHARTS, dtype=jnp.float32)[None, :, None, None, None]
    row = jnp.arange(ROWS, dtype=jnp.float32)[None, None, :, None, None]
    level = (chart * ROWS + row) / (CHARTS * ROWS)
    scale = 10.0 ** (level - 0.5)
    values = jnp.clip(jax.random.normal(noise_key, shape, jnp.float32), -4.0, 4.0) * scale
    return values.astype(jnp.bfloat16)


def shard_levels(stream_key, shape, cuts, least, high):
    def one(position, blocks):
        draws = jax.random.uniform(jax.random.fold_in(jax.random.fold_in(stream_key, 6), position), (blocks,), jnp.float32, least / len(cuts), high / len(cuts))
        return jnp.repeat(jnp.exp(draws), shape[position] // blocks).reshape((-1,) + (1,) * (len(shape) - position - 1))

    loudness = one(*cuts[0])
    for cut in cuts[1:]:
        loudness = loudness * one(*cut)
    return loudness


def scatter_about(own_key, shape, scale, reach, cuts=(), kind=jnp.bfloat16):
    values = jax.random.normal(own_key, shape, jnp.float32) * scale
    if len(cuts) > 0:
        values = shard_levels(own_key, shape, cuts, -0.22, 0.18) * values
    return jnp.clip(values, min=-reach, max=reach).astype(kind)


def setup_inputs(seed: int = 0) -> dict:
    seeds = jax.random.split(jax.random.key(seed), 7)
    activations = scatter_about(seeds[0], (FRAMES, CHARTS, ROWS, CH, COLS), 1.0, 6.0, ((0, 2), (1, 2), (2, 8)))
    upstream = draw_upstream(jax.random.fold_in(seeds[6], 71), 0)
    hex_weight = scatter_about(seeds[2], (7, CH, CH), (7 * CH) ** -0.5, 0.25)
    time_weight = scatter_about(seeds[3], (3, CH, CH), (3 * CH) ** -0.5, 0.4375)
    left_map = jax.vmap(lambda own: jax.random.permutation(own, ROWS))(jax.random.split(seeds[4], CHARTS)).reshape((CHARTS, ROWS)).astype(jnp.int32)
    right_map = jax.vmap(lambda own: jax.random.permutation(own, ROWS))(jax.random.split(seeds[5], CHARTS)).reshape((CHARTS, ROWS)).astype(jnp.int32)
    return {"activations": activations, "upstream": upstream, "hex_weight": hex_weight, "time_weight": time_weight, "left_map": left_map, "right_map": right_map}


OFFSETS = ((0, 0), (0, 1), (0, -1), (1, 0), (-1, 0), (1, -1), (-1, 1))
HIGHEST = lax.Precision.HIGHEST


def silu_slope(hidden):
    sigmoid = jax.nn.sigmoid(hidden)
    return sigmoid * (1.0 + hidden * (1.0 - sigmoid))


def pick_rows(strip, rows):
    return jnp.take(strip, rows, axis=1)


def place_rows(rows, values):
    return jnp.zeros((FRAMES, ROWS, CH), jnp.float32).at[:, rows].set(values)


def reference(activations, upstream, hex_weight, time_weight, left_map, right_map):
    hex_float = hex_weight.astype(jnp.float32)
    time_float = time_weight.astype(jnp.float32)
    prev_right = jnp.roll(activations[..., COLS - 1], 1, axis=1)
    next_left = jnp.roll(activations[..., 0], -1, axis=1)
    ghost_left = jax.vmap(pick_rows, in_axes=(1, 0), out_axes=1)(prev_right, left_map)
    ghost_right = jax.vmap(pick_rows, in_axes=(1, 0), out_axes=1)(next_left, right_map)

    def per_chart(inputs):
        field, cotangent, left_col, right_col = inputs
        widened = jnp.concatenate([left_col[..., None], field, right_col[..., None]], axis=-1)
        padded = jnp.pad(widened, ((0, 0), (1, 1), (0, 0), (0, 0))).astype(jnp.float32)
        hidden = jnp.zeros((FRAMES, ROWS, CH, COLS), jnp.float32)
        for number, (step_row, step_col) in enumerate(OFFSETS):
            window = padded[:, 1 + step_row:1 + step_row + ROWS, :, 1 + step_col:1 + step_col + COLS]
            hidden = hidden + jnp.einsum("frcx,cd->frdx", window, hex_float[number], precision=HIGHEST)
        active = jax.nn.silu(hidden).astype(jnp.bfloat16)
        active = lax.optimization_barrier(active).astype(jnp.float32)
        framed = jnp.pad(cotangent.astype(jnp.float32), ((1, 1), (0, 0), (0, 0), (0, 0)))
        grad_act = jnp.zeros((FRAMES, ROWS, CH, COLS), jnp.float32)
        time_terms = []
        for number in range(3):
            shifted = framed[2 - number:2 - number + FRAMES]
            grad_act = grad_act + jnp.einsum("frdx,cd->frcx", shifted, time_float[number], precision=HIGHEST)
            time_terms.append(jnp.einsum("frcx,frdx->cd", active, shifted, precision=HIGHEST))
        grad_pre = (grad_act * silu_slope(hidden)).astype(jnp.bfloat16)
        grad_pre = lax.optimization_barrier(grad_pre).astype(jnp.float32)
        spread = jnp.zeros((FRAMES, ROWS + 2, CH, COLS + 2), jnp.float32)
        hex_terms = []
        for number, (step_row, step_col) in enumerate(OFFSETS):
            window = padded[:, 1 + step_row:1 + step_row + ROWS, :, 1 + step_col:1 + step_col + COLS]
            hex_terms.append(jnp.einsum("frcx,frdx->cd", window, grad_pre, precision=HIGHEST))
            spread = spread.at[:, 1 + step_row:1 + step_row + ROWS, :, 1 + step_col:1 + step_col + COLS].add(
                jnp.einsum("frdx,cd->frcx", grad_pre, hex_float[number], precision=HIGHEST))
        total = cotangent.astype(jnp.float32) + spread[:, 1:ROWS + 1, :, 1:COLS + 1]
        return (total[..., 1:COLS - 1].astype(jnp.bfloat16), total[..., 0], total[..., COLS - 1],
                spread[:, 1:ROWS + 1, :, 0], spread[:, 1:ROWS + 1, :, COLS + 1],
                jnp.stack(hex_terms), jnp.stack(time_terms))

    moved = (jnp.moveaxis(activations, 1, 0), jnp.moveaxis(upstream, 1, 0),
             jnp.moveaxis(ghost_left, 1, 0), jnp.moveaxis(ghost_right, 1, 0))
    middle, first_col, last_col, left_grad, right_grad, hex_parts, time_parts = lax.map(per_chart, moved)
    last_col = last_col + jnp.roll(jax.vmap(place_rows)(left_map, left_grad), -1, axis=0)
    first_col = first_col + jnp.roll(jax.vmap(place_rows)(right_map, right_grad), 1, axis=0)
    result = jnp.concatenate([first_col.astype(jnp.bfloat16)[..., None], middle,
                              last_col.astype(jnp.bfloat16)[..., None]], axis=-1)
    return (jnp.moveaxis(result, 0, 1), jnp.sum(hex_parts, axis=0), jnp.sum(time_parts, axis=0))
```

```python
import jax
import jax.numpy as jnp
from jax import lax
from jax.experimental import pallas as pl
from jax.experimental.pallas import tpu as pltpu
from jax.sharding import PartitionSpec as P

OFFSETS = ((0, 0), (0, 1), (0, -1), (1, 0), (-1, 0), (1, -1), (-1, 1))
ANY = pl.BlockSpec(memory_space=pl.ANY)
VMEM = pl.BlockSpec(memory_space=pltpu.VMEM)


def remote(src, dst, send_sem, recv_sem, device_id):
    return pltpu.make_async_remote_copy(
        src_ref=src,
        dst_ref=dst,
        send_sem=send_sem,
        recv_sem=recv_sem,
        device_id=device_id,
        device_id_type=pl.DeviceIdType.MESH,
    )


def line_copies(axis, to_next, at_next, to_prev, at_prev, send, recv):
    me, size = lax.axis_index(axis), lax.axis_size(axis)
    up = remote(to_next, at_next, send.at[0], recv.at[0], {axis: lax.rem(me + 1, size)})
    down = remote(to_prev, at_prev, send.at[1], recv.at[1], {axis: lax.rem(me + size - 1, size)})

    def start():
        pl.when(me < size - 1)(up.start)
        pl.when(me > 0)(down.start)

    def wait():
        pl.when(me < size - 1)(up.wait_send)
        pl.when(me > 0)(down.wait_send)
        pl.when(me > 0)(up.wait_recv)
        pl.when(me < size - 1)(down.wait_recv)

    return start, wait


def seam_copies(strips, gathered, send, recv):
    me, tiles = lax.axis_index("tile"), lax.axis_size("tile")
    chart, charts = lax.axis_index("diamond"), lax.axis_size("diamond")
    sides = (lax.rem(chart + 1, charts), lax.rem(chart + charts - 1, charts))
    copies = []
    for step in range(tiles):
        other = lax.rem(me + step, tiles)
        for side in range(2):
            copies.append(
                remote(
                    strips.at[side],
                    gathered.at[side, me],
                    send.at[side, step],
                    recv.at[side, me],
                    {"diamond": sides[side], "tile": other},
                )
            )

    def start():
        for copy in copies:
            copy.start()

    def wait():
        for copy in copies:
            copy.wait_send()
        for side in range(2):
            for number in range(tiles):
                remote(
                    strips.at[side],
                    gathered.at[side, number],
                    send.at[side, 0],
                    recv.at[side, number],
                    {"diamond": sides[side], "tile": me},
                ).wait_recv()

    return start, wait


def first_exchange(
    strips, field, cotangent, gathered, above, below, before, after,
    seam_send, seam_recv, row_send, row_recv, frame_send, frame_recv,
):
    rows, frames = field.shape[1], field.shape[0]
    parts = (
        seam_copies(strips, gathered, seam_send, seam_recv),
        line_copies("tile", field.at[:, rows - 1], above, field.at[:, 0], below, row_send, row_recv),
        line_copies(
            "tm", cotangent.at[frames - 1], before, cotangent.at[0], after, frame_send, frame_recv
        ),
    )
    for start, _ in parts:
        start()
    for _, wait in parts:
        wait()


def last_exchange(
    strips, up_row, down_row, terms, gathered, above, below, sums,
    seam_send, seam_recv, row_send, row_recv,
    scattered, scatter_send, scatter_recv, group, group_send, group_recv, out_send, out_recv,
):
    me, tiles = lax.axis_index("tile"), lax.axis_size("tile")
    charts, lines = lax.axis_size("diamond"), lax.axis_size("tm")
    mine = lax.axis_index("tm") * charts + lax.axis_index("diamond")
    size = lines * charts

    def tile_copy(src, dst, send, recv, step):
        return remote(src, dst, send.at[step], recv, {"tile": lax.rem(me + step, tiles)})

    first = [
        tile_copy(
            terms.at[lax.rem(me + step, tiles)], scattered.at[me], scatter_send,
            scatter_recv.at[me], step,
        )
        for step in range(1, tiles)
    ]
    for copy in first:
        copy.start()
    parts = (
        seam_copies(strips, gathered, seam_send, seam_recv),
        line_copies("tile", down_row, above, up_row, below, row_send, row_recv),
    )
    for start, _ in parts:
        start()
    total = terms[me]
    for step in range(1, tiles):
        other = lax.rem(me + step, tiles)
        tile_copy(
            terms.at[other], scattered.at[other], scatter_send, scatter_recv.at[other], step
        ).wait_recv()
        total = total + scattered[other]
    group[mine] = total
    second = []
    for step in range(1, size):
        other = lax.rem(mine + step, size)
        target = {"tm": other // charts, "diamond": lax.rem(other, charts)}
        copy = remote(
            group.at[mine], group.at[mine], group_send.at[step], group_recv.at[mine], target
        )
        copy.start()
        second.append(copy)
    for step in range(1, size):
        other = lax.rem(mine + step, size)
        target = {"tm": other // charts, "diamond": lax.rem(other, charts)}
        remote(
            group.at[other], group.at[other], group_send.at[step], group_recv.at[other], target
        ).wait_recv()
    total = group[0]
    for number in range(1, size):
        total = total + group[number]
    sums[me] = total
    third = [
        tile_copy(sums.at[me], sums.at[me], out_send, out_recv.at[me], step)
        for step in range(1, tiles)
    ]
    for copy in third:
        copy.start()
    for step in range(1, tiles):
        other = lax.rem(me + step, tiles)
        tile_copy(sums.at[other], sums.at[other], out_send, out_recv.at[other], step).wait_recv()
    for copy in first + second + third:
        copy.wait_send()
    for _, wait in parts:
        wait()


def exchange_start(strips, field, cotangent):
    frames, rows, channels, columns = field.shape
    tiles = lax.axis_size("tile")
    dma = pltpu.SemaphoreType.DMA
    kind = field.dtype
    line = jax.ShapeDtypeStruct((frames, channels, columns), kind)
    frame = jax.ShapeDtypeStruct((rows, channels, columns), kind)
    return pl.pallas_call(
        first_exchange,
        out_shape=(
            jax.ShapeDtypeStruct((2, tiles) + strips.shape[1:], kind), line, line, frame, frame,
        ),
        in_specs=[ANY] * 3,
        out_specs=(ANY,) * 5,
        scratch_shapes=[
            dma((2, tiles)), dma((2, tiles)), dma((2,)), dma((2,)), dma((2,)), dma((2,)),
        ],
        compiler_params=pltpu.CompilerParams(has_side_effects=True),
        name="first_exchange",
    )(strips, field, cotangent)


def exchange_end(strips, up_row, down_row, terms):
    tiles = lax.axis_size("tile")
    size = lax.axis_size("tm") * lax.axis_size("diamond")
    dma = pltpu.SemaphoreType.DMA
    line = jax.ShapeDtypeStruct(up_row.shape, up_row.dtype)
    return pl.pallas_call(
        last_exchange,
        out_shape=(
            jax.ShapeDtypeStruct((2, tiles) + strips.shape[1:], strips.dtype), line, line,
            jax.ShapeDtypeStruct(terms.shape, terms.dtype),
        ),
        in_specs=[ANY, ANY, ANY, VMEM],
        out_specs=(ANY, ANY, ANY, VMEM),
        scratch_shapes=[
            dma((2, tiles)), dma((2, tiles)), dma((2,)), dma((2,)),
            pltpu.VMEM(terms.shape, terms.dtype), dma((tiles,)), dma((tiles,)),
            pltpu.VMEM((size,) + terms.shape[1:], terms.dtype), dma((size,)), dma((size,)),
            dma((tiles,)), dma((tiles,)),
        ],
        compiler_params=pltpu.CompilerParams(has_side_effects=True),
        name="last_exchange",
    )(strips, up_row, down_row, terms)


def silu_slope(hidden):
    sigmoid = jax.nn.sigmoid(hidden)
    return sigmoid * (1.0 + hidden * (1.0 - sigmoid))


def local_math(padded, framed, hex_weight, time_weight, frames, tile_rows, channels, columns):
    hidden = jnp.zeros((frames, tile_rows, channels, columns), jnp.float32)
    windows = [
        padded[:, 1 + a : 1 + a + tile_rows, :, 1 + b : 1 + b + columns] for a, b in OFFSETS
    ]
    for number in range(7):
        hidden = hidden + jnp.einsum(
            "frcx,cd->frdx", windows[number], hex_weight[number],
            preferred_element_type=jnp.float32,
        )
    active = jax.nn.silu(hidden).astype(jnp.bfloat16)
    grad_act = jnp.zeros((frames, tile_rows, channels, columns), jnp.float32)
    time_terms = []
    for number in range(3):
        shifted = framed[2 - number : 2 - number + frames]
        grad_act = grad_act + jnp.einsum(
            "frdx,cd->frcx", shifted, time_weight[number], preferred_element_type=jnp.float32
        )
        time_terms.append(
            jnp.einsum("frcx,frdx->cd", active, shifted, preferred_element_type=jnp.float32)
        )
    grad_wide = (grad_act * silu_slope(hidden)).astype(jnp.bfloat16)
    hex_terms = [
        jnp.einsum("frcx,frdx->cd", window, grad_wide, preferred_element_type=jnp.float32)
        for window in windows
    ]
    spread = None
    for number, (a, b) in enumerate(OFFSETS):
        term = jnp.einsum(
            "frdx,cd->frcx", grad_wide, hex_weight[number], preferred_element_type=jnp.float32
        )
        term = jnp.pad(term, ((0, 0), (1 + a, 1 - a), (0, 0), (1 + b, 1 - b)))
        spread = term if spread is None else spread + term
    return spread, jnp.stack(hex_terms + time_terms)


def shards(activations, upstream, hex_weight, time_weight, left_map, right_map):
    field = activations[:, 0]
    cotangent = upstream[:, 0]
    frames, tile_rows, channels, columns = field.shape
    chart, charts = lax.axis_index("diamond"), lax.axis_size("diamond")
    tile, tiles = lax.axis_index("tile"), lax.axis_size("tile")
    line, lines = lax.axis_index("tm"), lax.axis_size("tm")
    first_row = tile * tile_rows
    wide = tile_rows + 2
    strips = jnp.stack([field[..., columns - 1], field[..., 0]]).reshape(
        2, frames * tile_rows, channels
    )
    gathered, above, below, before, after = exchange_start(strips, field, cotangent)
    above = jnp.where(tile > 0, above, 0)
    below = jnp.where(tile < tiles - 1, below, 0)
    before = jnp.where(line > 0, before, 0)
    after = jnp.where(line < lines - 1, after, 0)

    def chart_rows(table, number):
        own = lax.dynamic_slice(table, (number, 0), (1, table.shape[1]))[0]
        return jnp.pad(own, (1, 1), constant_values=-1)

    every = jnp.arange(tiles * tile_rows)

    def ghost(strip, table):
        own = lax.dynamic_slice(chart_rows(table, chart), (first_row,), (wide,))
        pick = (own[:, None] == every[None, :]).astype(jnp.bfloat16)
        pick = pick.reshape(wide, tiles, tile_rows)
        strip = strip.reshape(tiles, frames, tile_rows, channels)
        return jnp.einsum("wtr,tfrc->fwc", pick, strip, preferred_element_type=jnp.float32).astype(
            jnp.bfloat16
        )

    ghost_left = ghost(gathered[0], left_map)
    ghost_right = ghost(gathered[1], right_map)
    rows = jnp.concatenate([above[:, None], field, below[:, None]], axis=1)
    padded = jnp.concatenate([ghost_left[..., None], rows, ghost_right[..., None]], axis=-1)
    framed = jnp.concatenate([before[None], cotangent, after[None]], axis=0)
    spread, terms = local_math(
        padded, framed, hex_weight, time_weight, frames, tile_rows, channels, columns
    )
    sent = spread.astype(jnp.bfloat16)
    strips = jnp.stack([sent[..., columns + 1], sent[..., 0]]).reshape(2, frames * wide, channels)
    count = terms.size // (tiles * 128)
    gathered, above, below, sums = exchange_end(
        strips, sent[:, 0, :, 1 : columns + 1], sent[:, wide - 1, :, 1 : columns + 1],
        terms.reshape(tiles, count, 128),
    )
    sums = sums.reshape(terms.shape)
    total = cotangent.astype(jnp.float32) + spread[:, 1 : tile_rows + 1, :, 1 : columns + 1]
    above = jnp.where(tile > 0, above, 0).astype(jnp.float32)
    below = jnp.where(tile < tiles - 1, below, 0).astype(jnp.float32)
    total = total + jnp.pad(above[:, None], ((0, 0), (0, tile_rows - 1), (0, 0), (0, 0)))
    total = total + jnp.pad(below[:, None], ((0, 0), (tile_rows - 1, 0), (0, 0), (0, 0)))
    own_rows = first_row + jnp.arange(tile_rows)
    source = (jnp.arange(tiles)[:, None] * tile_rows + jnp.arange(wide)[None, :]).reshape(-1)

    def landing(strip, table, number):
        target = jnp.take(chart_rows(table, number), source)
        pick = (own_rows[:, None] == target[None, :]).astype(jnp.bfloat16)
        pick = pick.reshape(tile_rows, tiles, wide)
        strip = strip.reshape(tiles, frames, wide, channels)
        return jnp.einsum("rtw,tfwc->frc", pick, strip, preferred_element_type=jnp.float32)

    into_first = landing(gathered[0], right_map, lax.rem(chart + charts - 1, charts))
    into_last = landing(gathered[1], left_map, lax.rem(chart + 1, charts))
    column = jnp.arange(columns)
    total = total + jnp.where(column == 0, into_first[..., None], 0.0)
    total = total + jnp.where(column == columns - 1, into_last[..., None], 0.0)
    return total.astype(jnp.bfloat16)[:, None], sums[:7], sums[7:]


def solution(mesh):
    whole = P("tm", "diamond", "tile", None, None)
    return jax.shard_map(
        shards,
        mesh=mesh,
        in_specs=(whole, whole, P(), P(), P(), P()),
        out_specs=(whole, P(), P()),
        check_vma=False,
    )
```

```python
import jax
import jax.numpy as jnp
from jax import lax
from jax.experimental import pallas as pl
from jax.experimental.pallas import tpu as pltpu
from jax.sharding import PartitionSpec as P

OFFSETS = ((0, 0), (0, 1), (0, -1), (1, 0), (-1, 0), (1, -1), (-1, 1))
ANY = pl.BlockSpec(memory_space=pl.ANY)
VMEM = pl.BlockSpec(memory_space=pltpu.VMEM)


def remote(src, dst, send_sem, recv_sem, device_id):
    return pltpu.make_async_remote_copy(
        src_ref=src,
        dst_ref=dst,
        send_sem=send_sem,
        recv_sem=recv_sem,
        device_id=device_id,
        device_id_type=pl.DeviceIdType.MESH,
    )


def line_copies(axis, to_next, at_next, to_prev, at_prev, send, recv):
    me, size = lax.axis_index(axis), lax.axis_size(axis)
    up = remote(to_next, at_next, send.at[0], recv.at[0], {axis: lax.rem(me + 1, size)})
    down = remote(to_prev, at_prev, send.at[1], recv.at[1], {axis: lax.rem(me + size - 1, size)})

    def start():
        pl.when(me < size - 1)(up.start)
        pl.when(me > 0)(down.start)

    def wait():
        pl.when(me < size - 1)(up.wait_send)
        pl.when(me > 0)(down.wait_send)
        pl.when(me > 0)(up.wait_recv)
        pl.when(me < size - 1)(down.wait_recv)

    return start, wait


def seam_copies(strips, gathered, send, recv):
    me, tiles = lax.axis_index("tile"), lax.axis_size("tile")
    chart, charts = lax.axis_index("diamond"), lax.axis_size("diamond")
    sides = (lax.rem(chart + 1, charts), lax.rem(chart + charts - 1, charts))
    parts = (slice(0, 2),) if charts == 2 else (slice(0, 1), slice(1, 2))

    def copy(part, step, source, target):
        return remote(
            strips.at[parts[part]],
            gathered.at[source, parts[part]],
            send.at[part, step],
            recv.at[part, source],
            {"diamond": sides[part], "tile": target},
        )

    copies = [
        copy(part, step, me, lax.rem(me + step, tiles))
        for step in range(tiles)
        for part in range(len(parts))
    ]

    def start():
        for one in copies:
            one.start()

    def wait():
        for one in copies:
            one.wait_send()
        for part in range(len(parts)):
            for number in range(tiles):
                copy(part, 0, number, me).wait_recv()

    return start, wait


def first_exchange(
    strips, field, cotangent, gathered, above, below, before, after,
    seam_send, seam_recv, row_send, row_recv, frame_send, frame_recv,
):
    rows, frames = field.shape[1], field.shape[0]
    parts = (
        seam_copies(strips, gathered, seam_send, seam_recv),
        line_copies("tile", field.at[:, rows - 1], above, field.at[:, 0], below, row_send, row_recv),
        line_copies(
            "tm", cotangent.at[frames - 1], before, cotangent.at[0], after, frame_send, frame_recv
        ),
    )
    for start, _ in parts:
        start()
    for _, wait in parts:
        wait()


def last_exchange(
    strips, up_row, down_row, terms, gathered, above, below, sums,
    seam_send, seam_recv, row_send, row_recv,
    scattered, scatter_send, scatter_recv, group, group_send, group_recv, out_send, out_recv,
):
    me, tiles = lax.axis_index("tile"), lax.axis_size("tile")
    charts, lines = lax.axis_size("diamond"), lax.axis_size("tm")
    mine = lax.axis_index("tm") * charts + lax.axis_index("diamond")
    size = lines * charts

    def tile_copy(src, dst, send, recv, step):
        return remote(src, dst, send.at[step], recv, {"tile": lax.rem(me + step, tiles)})

    first = [
        tile_copy(
            terms.at[lax.rem(me + step, tiles)], scattered.at[me], scatter_send,
            scatter_recv.at[me], step,
        )
        for step in range(1, tiles)
    ]
    for copy in first:
        copy.start()
    parts = (
        seam_copies(strips, gathered, seam_send, seam_recv),
        line_copies("tile", down_row, above, up_row, below, row_send, row_recv),
    )
    for start, _ in parts:
        start()
    total = terms[me]
    for step in range(1, tiles):
        other = lax.rem(me + step, tiles)
        tile_copy(
            terms.at[other], scattered.at[other], scatter_send, scatter_recv.at[other], step
        ).wait_recv()
        total = total + scattered[other]
    group[mine] = total
    second = []
    for step in range(1, size):
        other = lax.rem(mine + step, size)
        target = {"tm": other // charts, "diamond": lax.rem(other, charts)}
        copy = remote(
            group.at[mine], group.at[mine], group_send.at[step], group_recv.at[mine], target
        )
        copy.start()
        second.append(copy)
    for step in range(1, size):
        other = lax.rem(mine + step, size)
        target = {"tm": other // charts, "diamond": lax.rem(other, charts)}
        remote(
            group.at[other], group.at[other], group_send.at[step], group_recv.at[other], target
        ).wait_recv()
    total = group[0]
    for number in range(1, size):
        total = total + group[number]
    sums[me] = total
    third = [
        tile_copy(sums.at[me], sums.at[me], out_send, out_recv.at[me], step)
        for step in range(1, tiles)
    ]
    for copy in third:
        copy.start()
    for step in range(1, tiles):
        other = lax.rem(me + step, tiles)
        tile_copy(sums.at[other], sums.at[other], out_send, out_recv.at[other], step).wait_recv()
    for copy in first + second + third:
        copy.wait_send()
    for _, wait in parts:
        wait()


def exchange_start(strips, field, cotangent):
    frames, rows, channels, columns = field.shape
    tiles = lax.axis_size("tile")
    dma = pltpu.SemaphoreType.DMA
    kind = field.dtype
    line = jax.ShapeDtypeStruct((frames, channels, columns), kind)
    frame = jax.ShapeDtypeStruct((rows, channels, columns), kind)
    return pl.pallas_call(
        first_exchange,
        out_shape=(
            jax.ShapeDtypeStruct((tiles,) + strips.shape, kind), line, line, frame, frame,
        ),
        in_specs=[ANY] * 3,
        out_specs=(ANY,) * 5,
        scratch_shapes=[
            dma((2, tiles)), dma((2, tiles)), dma((2,)), dma((2,)), dma((2,)), dma((2,)),
        ],
        compiler_params=pltpu.CompilerParams(has_side_effects=True),
        name="first_exchange",
    )(strips, field, cotangent)


def exchange_end(strips, up_row, down_row, terms):
    tiles = lax.axis_size("tile")
    size = lax.axis_size("tm") * lax.axis_size("diamond")
    dma = pltpu.SemaphoreType.DMA
    line = jax.ShapeDtypeStruct(up_row.shape, up_row.dtype)
    return pl.pallas_call(
        last_exchange,
        out_shape=(
            jax.ShapeDtypeStruct((tiles,) + strips.shape, strips.dtype), line, line,
            jax.ShapeDtypeStruct(terms.shape, terms.dtype),
        ),
        in_specs=[ANY, ANY, ANY, VMEM],
        out_specs=(ANY, ANY, ANY, VMEM),
        scratch_shapes=[
            dma((2, tiles)), dma((2, tiles)), dma((2,)), dma((2,)),
            pltpu.VMEM(terms.shape, terms.dtype), dma((tiles,)), dma((tiles,)),
            pltpu.VMEM((size,) + terms.shape[1:], terms.dtype), dma((size,)), dma((size,)),
            dma((tiles,)), dma((tiles,)),
        ],
        compiler_params=pltpu.CompilerParams(has_side_effects=True),
        name="last_exchange",
    )(strips, up_row, down_row, terms)


def silu_slope(hidden):
    sigmoid = jax.nn.sigmoid(hidden)
    return sigmoid * (1.0 + hidden * (1.0 - sigmoid))


def local_math(padded, framed, hex_weight, time_weight, frames, tile_rows, channels, columns):
    hidden = jnp.zeros((frames, tile_rows, channels, columns), jnp.float32)
    windows = [
        padded[:, 1 + a : 1 + a + tile_rows, :, 1 + b : 1 + b + columns] for a, b in OFFSETS
    ]
    for number in range(7):
        hidden = hidden + jnp.einsum(
            "frcx,cd->frdx", windows[number], hex_weight[number],
            preferred_element_type=jnp.float32,
        )
    active = jax.nn.silu(hidden).astype(jnp.bfloat16)
    grad_act = jnp.zeros((frames, tile_rows, channels, columns), jnp.float32)
    time_terms = []
    for number in range(3):
        shifted = framed[2 - number : 2 - number + frames]
        grad_act = grad_act + jnp.einsum(
            "frdx,cd->frcx", shifted, time_weight[number], preferred_element_type=jnp.float32
        )
        time_terms.append(
            jnp.einsum("frcx,frdx->cd", active, shifted, preferred_element_type=jnp.float32)
        )
    grad_wide = (grad_act * silu_slope(hidden)).astype(jnp.bfloat16)
    hex_terms = [
        jnp.einsum("frcx,frdx->cd", window, grad_wide, preferred_element_type=jnp.float32)
        for window in windows
    ]
    spread = None
    for number, (a, b) in enumerate(OFFSETS):
        term = jnp.einsum(
            "frdx,cd->frcx", grad_wide, hex_weight[number], preferred_element_type=jnp.float32
        )
        if b == 1:
            term = jnp.pad(term[..., :-1], ((0, 0), (0, 0), (0, 0), (1, 0)))
        if b == -1:
            term = jnp.pad(term[..., 1:], ((0, 0), (0, 0), (0, 0), (0, 1)))
        term = jnp.pad(term, ((0, 0), (1 + a, 1 - a), (0, 0), (0, 0)))
        spread = term if spread is None else spread + term
    seams = seam_columns(grad_wide)
    sides = []
    for side, b in ((0, 1), (1, -1)):
        seam = None
        for number, (a, _) in enumerate(OFFSETS):
            if OFFSETS[number][1] == b:
                term = jnp.einsum(
                    "frd,cd->frc", seams[side], hex_weight[number],
                    preferred_element_type=jnp.float32,
                )
                term = jnp.pad(term, ((0, 0), (1 + a, 1 - a), (0, 0)))
                seam = term if seam is None else seam + term
        sides.append(seam)
    return spread, jnp.stack(sides).astype(jnp.bfloat16), jnp.stack(hex_terms + time_terms)


def seam_columns(block):
    columns = block.shape[-1]
    pick = jnp.array([columns - 1, 0])[:, None] == jnp.arange(columns)[None, :]
    return jnp.einsum(
        "sx,frcx->sfrc", pick.astype(block.dtype), block, preferred_element_type=jnp.float32
    ).astype(block.dtype)


def shards(activations, upstream, hex_weight, time_weight, left_map, right_map):
    field = activations[:, 0]
    cotangent = upstream[:, 0]
    frames, tile_rows, channels, columns = field.shape
    chart, charts = lax.axis_index("diamond"), lax.axis_size("diamond")
    tile, tiles = lax.axis_index("tile"), lax.axis_size("tile")
    line, lines = lax.axis_index("tm"), lax.axis_size("tm")
    first_row = tile * tile_rows
    wide = tile_rows + 2
    strips = seam_columns(field).reshape(2, frames * tile_rows, channels)
    gathered, above, below, before, after = exchange_start(strips, field, cotangent)
    above = jnp.where(tile > 0, above, 0)
    below = jnp.where(tile < tiles - 1, below, 0)
    before = jnp.where(line > 0, before, 0)
    after = jnp.where(line < lines - 1, after, 0)

    def chart_rows(table, number):
        own = lax.dynamic_slice(table, (number, 0), (1, table.shape[1]))[0]
        return jnp.pad(own, (1, 1), constant_values=-1)

    every = jnp.arange(tiles * tile_rows)

    def ghost(strip, table):
        own = lax.dynamic_slice(chart_rows(table, chart), (first_row,), (wide,))
        pick = (own[:, None] == every[None, :]).astype(jnp.bfloat16)
        pick = pick.reshape(wide, tiles, tile_rows)
        strip = strip.reshape(tiles, frames, tile_rows, channels)
        return jnp.einsum("wtr,tfrc->fwc", pick, strip, preferred_element_type=jnp.float32).astype(
            jnp.bfloat16
        )

    ghost_left = ghost(gathered[:, 0], left_map)
    ghost_right = ghost(gathered[:, 1], right_map)
    rows = jnp.concatenate([above[:, None], field, below[:, None]], axis=1)
    padded = jnp.concatenate([ghost_left[..., None], rows, ghost_right[..., None]], axis=-1)
    framed = jnp.concatenate([before[None], cotangent, after[None]], axis=0)
    spread, seams, terms = local_math(
        padded, framed, hex_weight, time_weight, frames, tile_rows, channels, columns
    )
    strips = seams.reshape(2, frames * wide, channels)
    count = terms.size // (tiles * 128)
    gathered, above, below, sums = exchange_end(
        strips, spread[:, 0].astype(jnp.bfloat16), spread[:, wide - 1].astype(jnp.bfloat16),
        terms.reshape(tiles, count, 128),
    )
    sums = sums.reshape(terms.shape)
    total = cotangent.astype(jnp.float32) + spread[:, 1 : tile_rows + 1]
    above = jnp.where(tile > 0, above, 0).astype(jnp.float32)
    below = jnp.where(tile < tiles - 1, below, 0).astype(jnp.float32)
    total = total + jnp.pad(above[:, None], ((0, 0), (0, tile_rows - 1), (0, 0), (0, 0)))
    total = total + jnp.pad(below[:, None], ((0, 0), (tile_rows - 1, 0), (0, 0), (0, 0)))
    own_rows = first_row + jnp.arange(tile_rows)

    def landing(strip, table, number):
        target = chart_rows(table, number)
        inner = target[1:-1].reshape(tiles, tile_rows)
        prior = target[:-2].reshape(tiles, tile_rows)[:, :1]
        later = target[2:].reshape(tiles, tile_rows)[:, -1:]
        target = jnp.concatenate([prior, inner, later], axis=1)
        pick = (own_rows[:, None, None] == target[None]).astype(jnp.bfloat16)
        strip = strip.reshape(tiles, frames, wide, channels)
        return jnp.einsum("rtw,tfwc->frc", pick, strip, preferred_element_type=jnp.float32)

    into_first = landing(gathered[:, 0], right_map, lax.rem(chart + charts - 1, charts))
    into_last = landing(gathered[:, 1], left_map, lax.rem(chart + 1, charts))
    column = jnp.arange(columns)
    total = total + jnp.where(column == 0, into_first[..., None], 0.0)
    total = total + jnp.where(column == columns - 1, into_last[..., None], 0.0)
    return total.astype(jnp.bfloat16)[:, None], sums[:7], sums[7:]


def solution(mesh):
    whole = P("tm", "diamond", "tile", None, None)
    return jax.shard_map(
        shards,
        mesh=mesh,
        in_specs=(whole, whole, P(), P(), P(), P()),
        out_specs=(whole, P(), P()),
        check_vma=False,
    )
```

```python
import jax
import jax.numpy as jnp
from jax import lax
from jax.experimental import pallas as pl
from jax.experimental.pallas import tpu as pltpu
from jax.sharding import PartitionSpec as P

OFFSETS = ((0, 0), (0, 1), (0, -1), (1, 0), (-1, 0), (1, -1), (-1, 1))
ANY = pl.BlockSpec(memory_space=pl.ANY)
VMEM = pl.BlockSpec(memory_space=pltpu.VMEM)


def remote(src, dst, send_sem, recv_sem, device_id):
    return pltpu.make_async_remote_copy(
        src_ref=src,
        dst_ref=dst,
        send_sem=send_sem,
        recv_sem=recv_sem,
        device_id=device_id,
        device_id_type=pl.DeviceIdType.MESH,
    )


def meet(whole_tile, whole_group):
    me, tiles = lax.axis_index("tile"), lax.axis_size("tile")
    chart, charts = lax.axis_index("diamond"), lax.axis_size("diamond")
    line, lines = lax.axis_index("tm"), lax.axis_size("tm")
    mine, size = line * charts + chart, lines * charts
    partners = [
        {"diamond": lax.rem(chart + turn, charts), "tile": lax.rem(me + step, tiles)}
        for turn in sorted({1, charts - 1})
        for step in range(tiles)
    ]
    steps = range(1, tiles) if whole_tile else sorted({1, tiles - 1})
    partners += [{"tile": lax.rem(me + step, tiles)} for step in steps]
    if whole_group:
        others = [lax.rem(mine + step, size) for step in range(1, size)]
        partners += [{"tm": one // charts, "diamond": lax.rem(one, charts)} for one in others]
    else:
        partners += [{"tm": lax.rem(line + step, lines)} for step in sorted({1, lines - 1})]
    barrier = pltpu.get_barrier_semaphore()
    for partner in partners:
        pl.semaphore_signal(
            barrier, inc=1, device_id=partner, device_id_type=pl.DeviceIdType.MESH
        )
    pl.semaphore_wait(barrier, len(partners))


def line_copies(axis, to_next, at_next, to_prev, at_prev, send, recv):
    me, size = lax.axis_index(axis), lax.axis_size(axis)
    up = remote(to_next, at_next, send.at[0], recv.at[0], {axis: lax.rem(me + 1, size)})
    down = remote(to_prev, at_prev, send.at[1], recv.at[1], {axis: lax.rem(me + size - 1, size)})

    def start():
        pl.when(me < size - 1)(up.start)
        pl.when(me > 0)(down.start)

    def wait():
        pl.when(me < size - 1)(up.wait_send)
        pl.when(me > 0)(down.wait_send)
        pl.when(me > 0)(up.wait_recv)
        pl.when(me < size - 1)(down.wait_recv)

    return start, wait


def seam_copies(strips, gathered, send, recv):
    me, tiles = lax.axis_index("tile"), lax.axis_size("tile")
    chart, charts = lax.axis_index("diamond"), lax.axis_size("diamond")
    sides = (lax.rem(chart + 1, charts), lax.rem(chart + charts - 1, charts))
    parts = (slice(0, 2),) if charts == 2 else (slice(0, 1), slice(1, 2))

    def copy(part, step, source, target):
        return remote(
            strips.at[parts[part]],
            gathered.at[source, parts[part]],
            send.at[part, step],
            recv.at[part, source],
            {"diamond": sides[part], "tile": target},
        )

    copies = [
        copy(part, step, me, lax.rem(me + step, tiles))
        for step in range(tiles)
        for part in range(len(parts))
    ]

    def start():
        for one in copies:
            one.start()

    def wait():
        for one in copies:
            one.wait_send()
        for part in range(len(parts)):
            for number in range(tiles):
                copy(part, 0, number, me).wait_recv()

    return start, wait


def first_exchange(
    strips, field, cotangent, gathered, above, below, before, after,
    seam_send, seam_recv, row_send, row_recv, frame_send, frame_recv,
):
    meet(False, False)
    rows, frames = field.shape[1], field.shape[0]
    parts = (
        seam_copies(strips, gathered, seam_send, seam_recv),
        line_copies("tile", field.at[:, rows - 1], above, field.at[:, 0], below, row_send, row_recv),
        line_copies(
            "tm", cotangent.at[frames - 1], before, cotangent.at[0], after, frame_send, frame_recv
        ),
    )
    for start, _ in parts:
        start()
    for _, wait in parts:
        wait()


def last_exchange(
    strips, up_row, down_row, terms, gathered, above, below, sums,
    seam_send, seam_recv, row_send, row_recv,
    scattered, scatter_send, scatter_recv, group, group_send, group_recv, out_send, out_recv,
):
    meet(True, True)
    me, tiles = lax.axis_index("tile"), lax.axis_size("tile")
    charts, lines = lax.axis_size("diamond"), lax.axis_size("tm")
    mine = lax.axis_index("tm") * charts + lax.axis_index("diamond")
    size = lines * charts

    def tile_copy(src, dst, send, recv, step):
        return remote(src, dst, send.at[step], recv, {"tile": lax.rem(me + step, tiles)})

    first = [
        tile_copy(
            terms.at[lax.rem(me + step, tiles)], scattered.at[me], scatter_send,
            scatter_recv.at[me], step,
        )
        for step in range(1, tiles)
    ]
    for copy in first:
        copy.start()
    parts = (
        seam_copies(strips, gathered, seam_send, seam_recv),
        line_copies("tile", down_row, above, up_row, below, row_send, row_recv),
    )
    for start, _ in parts:
        start()
    total = terms[me]
    for step in range(1, tiles):
        other = lax.rem(me + step, tiles)
        tile_copy(
            terms.at[other], scattered.at[other], scatter_send, scatter_recv.at[other], step
        ).wait_recv()
        total = total + scattered[other]
    group[mine] = total
    second = []
    for step in range(1, size):
        other = lax.rem(mine + step, size)
        target = {"tm": other // charts, "diamond": lax.rem(other, charts)}
        copy = remote(
            group.at[mine], group.at[mine], group_send.at[step], group_recv.at[mine], target
        )
        copy.start()
        second.append(copy)
    for step in range(1, size):
        other = lax.rem(mine + step, size)
        target = {"tm": other // charts, "diamond": lax.rem(other, charts)}
        remote(
            group.at[other], group.at[other], group_send.at[step], group_recv.at[other], target
        ).wait_recv()
    total = group[0]
    for number in range(1, size):
        total = total + group[number]
    sums[me] = total
    third = [
        tile_copy(sums.at[me], sums.at[me], out_send, out_recv.at[me], step)
        for step in range(1, tiles)
    ]
    for copy in third:
        copy.start()
    for step in range(1, tiles):
        other = lax.rem(me + step, tiles)
        tile_copy(sums.at[other], sums.at[other], out_send, out_recv.at[other], step).wait_recv()
    for copy in first + second + third:
        copy.wait_send()
    for _, wait in parts:
        wait()


def exchange_start(strips, field, cotangent):
    frames, rows, channels, columns = field.shape
    tiles = lax.axis_size("tile")
    dma = pltpu.SemaphoreType.DMA
    kind = field.dtype
    line = jax.ShapeDtypeStruct((frames, channels, columns), kind)
    frame = jax.ShapeDtypeStruct((rows, channels, columns), kind)
    return pl.pallas_call(
        first_exchange,
        out_shape=(
            jax.ShapeDtypeStruct((tiles,) + strips.shape, kind), line, line, frame, frame,
        ),
        in_specs=[ANY] * 3,
        out_specs=(ANY,) * 5,
        scratch_shapes=[
            dma((2, tiles)), dma((2, tiles)), dma((2,)), dma((2,)), dma((2,)), dma((2,)),
        ],
        compiler_params=pltpu.CompilerParams(collective_id=0, has_side_effects=True),
        name="first_exchange",
    )(strips, field, cotangent)


def exchange_end(strips, up_row, down_row, terms):
    tiles = lax.axis_size("tile")
    size = lax.axis_size("tm") * lax.axis_size("diamond")
    dma = pltpu.SemaphoreType.DMA
    line = jax.ShapeDtypeStruct(up_row.shape, up_row.dtype)
    return pl.pallas_call(
        last_exchange,
        out_shape=(
            jax.ShapeDtypeStruct((tiles,) + strips.shape, strips.dtype), line, line,
            jax.ShapeDtypeStruct(terms.shape, terms.dtype),
        ),
        in_specs=[ANY, ANY, ANY, VMEM],
        out_specs=(ANY, ANY, ANY, VMEM),
        scratch_shapes=[
            dma((2, tiles)), dma((2, tiles)), dma((2,)), dma((2,)),
            pltpu.VMEM(terms.shape, terms.dtype), dma((tiles,)), dma((tiles,)),
            pltpu.VMEM((size,) + terms.shape[1:], terms.dtype), dma((size,)), dma((size,)),
            dma((tiles,)), dma((tiles,)),
        ],
        compiler_params=pltpu.CompilerParams(collective_id=1, has_side_effects=True),
        name="last_exchange",
    )(strips, up_row, down_row, terms)


def silu_slope(hidden):
    sigmoid = jax.nn.sigmoid(hidden)
    return sigmoid * (1.0 + hidden * (1.0 - sigmoid))


def local_math(padded, framed, hex_weight, time_weight, frames, tile_rows, channels, columns):
    hidden = jnp.zeros((frames, tile_rows, channels, columns), jnp.float32)
    windows = [
        padded[:, 1 + a : 1 + a + tile_rows, :, 1 + b : 1 + b + columns] for a, b in OFFSETS
    ]
    for number in range(7):
        hidden = hidden + jnp.einsum(
            "frcx,cd->frdx", windows[number], hex_weight[number],
            preferred_element_type=jnp.float32,
        )
    active = jax.nn.silu(hidden).astype(jnp.bfloat16)
    grad_act = jnp.zeros((frames, tile_rows, channels, columns), jnp.float32)
    time_terms = []
    for number in range(3):
        shifted = framed[2 - number : 2 - number + frames]
        grad_act = grad_act + jnp.einsum(
            "frdx,cd->frcx", shifted, time_weight[number], preferred_element_type=jnp.float32
        )
        time_terms.append(
            jnp.einsum("frcx,frdx->cd", active, shifted, preferred_element_type=jnp.float32)
        )
    grad_wide = (grad_act * silu_slope(hidden)).astype(jnp.bfloat16)
    hex_terms = [
        jnp.einsum("frcx,frdx->cd", window, grad_wide, preferred_element_type=jnp.float32)
        for window in windows
    ]
    spread = None
    for number, (a, b) in enumerate(OFFSETS):
        term = jnp.einsum(
            "frdx,cd->frcx", grad_wide, hex_weight[number], preferred_element_type=jnp.float32
        )
        if b == 1:
            term = jnp.pad(term[..., :-1], ((0, 0), (0, 0), (0, 0), (1, 0)))
        if b == -1:
            term = jnp.pad(term[..., 1:], ((0, 0), (0, 0), (0, 0), (0, 1)))
        term = jnp.pad(term, ((0, 0), (1 + a, 1 - a), (0, 0), (0, 0)))
        spread = term if spread is None else spread + term
    seams = seam_columns(grad_wide)
    sides = []
    for side, b in ((0, 1), (1, -1)):
        seam = None
        for number, (a, _) in enumerate(OFFSETS):
            if OFFSETS[number][1] == b:
                term = jnp.einsum(
                    "frd,cd->frc", seams[side], hex_weight[number],
                    preferred_element_type=jnp.float32,
                )
                term = jnp.pad(term, ((0, 0), (1 + a, 1 - a), (0, 0)))
                seam = term if seam is None else seam + term
        sides.append(seam)
    return spread, jnp.stack(sides).astype(jnp.bfloat16), jnp.stack(
        [
            jnp.concatenate(pair, axis=-1)
            for pair in zip(hex_terms[:5], hex_terms[5:] + time_terms)
        ]
    )


def seam_columns(block):
    return jnp.stack([block[..., block.shape[-1] - 1], block[..., 0]])


def shards(activations, upstream, hex_weight, time_weight, left_map, right_map):
    field = activations[:, 0]
    cotangent = upstream[:, 0]
    frames, tile_rows, channels, columns = field.shape
    chart, charts = lax.axis_index("diamond"), lax.axis_size("diamond")
    tile, tiles = lax.axis_index("tile"), lax.axis_size("tile")
    line, lines = lax.axis_index("tm"), lax.axis_size("tm")
    first_row = tile * tile_rows
    wide = tile_rows + 2
    strips = seam_columns(field).reshape(2, frames * tile_rows, channels)
    gathered, above, below, before, after = exchange_start(strips, field, cotangent)
    above = jnp.where(tile > 0, above, 0)
    below = jnp.where(tile < tiles - 1, below, 0)
    before = jnp.where(line > 0, before, 0)
    after = jnp.where(line < lines - 1, after, 0)

    def chart_rows(table, number):
        own = lax.dynamic_slice(table, (number, 0), (1, table.shape[1]))[0]
        return jnp.pad(own, (1, 1), constant_values=-1)

    every = jnp.arange(tiles * tile_rows)

    def ghost(strip, table):
        own = lax.dynamic_slice(chart_rows(table, chart), (first_row,), (wide,))
        pick = (own[:, None] == every[None, :]).astype(jnp.bfloat16)
        pick = pick.reshape(wide, tiles, tile_rows)
        strip = strip.reshape(tiles, frames, tile_rows, channels)
        return jnp.einsum("wtr,tfrc->fwc", pick, strip, preferred_element_type=jnp.float32).astype(
            jnp.bfloat16
        )

    ghost_left = ghost(gathered[:, 0], left_map)
    ghost_right = ghost(gathered[:, 1], right_map)
    rows = jnp.concatenate([above[:, None], field, below[:, None]], axis=1)
    padded = jnp.concatenate([ghost_left[..., None], rows, ghost_right[..., None]], axis=-1)
    framed = jnp.concatenate([before[None], cotangent, after[None]], axis=0)
    spread, seams, terms = local_math(
        padded, framed, hex_weight, time_weight, frames, tile_rows, channels, columns
    )
    strips = seams.reshape(2, frames * wide, channels)
    count = terms.size // (tiles * 128)
    gathered, above, below, sums = exchange_end(
        strips, spread[:, 0].astype(jnp.bfloat16), spread[:, wide - 1].astype(jnp.bfloat16),
        terms.reshape(tiles, count, 128),
    )
    sums = sums.reshape(terms.shape)
    total = cotangent.astype(jnp.float32) + spread[:, 1 : tile_rows + 1]
    above = jnp.where(tile > 0, above, 0).astype(jnp.float32)
    below = jnp.where(tile < tiles - 1, below, 0).astype(jnp.float32)
    total = total + jnp.pad(above[:, None], ((0, 0), (0, tile_rows - 1), (0, 0), (0, 0)))
    total = total + jnp.pad(below[:, None], ((0, 0), (tile_rows - 1, 0), (0, 0), (0, 0)))
    own_rows = first_row + jnp.arange(tile_rows)

    def landing(strip, table, number):
        target = chart_rows(table, number)
        inner = target[1:-1].reshape(tiles, tile_rows)
        prior = target[:-2].reshape(tiles, tile_rows)[:, :1]
        later = target[2:].reshape(tiles, tile_rows)[:, -1:]
        target = jnp.concatenate([prior, inner, later], axis=1)
        pick = (own_rows[:, None, None] == target[None]).astype(jnp.bfloat16)
        strip = strip.reshape(tiles, frames, wide, channels)
        return jnp.einsum("rtw,tfwc->frc", pick, strip, preferred_element_type=jnp.float32)

    into_first = landing(gathered[:, 0], right_map, lax.rem(chart + charts - 1, charts))
    into_last = landing(gathered[:, 1], left_map, lax.rem(chart + 1, charts))
    column = jnp.arange(columns)
    total = total + jnp.where(column == 0, into_first[..., None], 0.0)
    total = total + jnp.where(column == columns - 1, into_last[..., None], 0.0)
    ahead, behind = sums[..., :channels], sums[..., channels:]
    grad_hex = jnp.concatenate([ahead, behind[:2]], axis=0)
    return total.astype(jnp.bfloat16)[:, None], grad_hex, behind[2:]


def solution(mesh):
    whole = P("tm", "diamond", "tile", None, None)
    return jax.shard_map(
        shards,
        mesh=mesh,
        in_specs=(whole, whole, P(), P(), P(), P()),
        out_specs=(whole, P(), P()),
        check_vma=False,
    )
```

```python
import jax
import jax.numpy as jnp
from jax import lax
from jax.experimental import pallas as pl
from jax.experimental.layout import Layout, with_layout_constraint
from jax.experimental.pallas import tpu as pltpu
from jax.sharding import PartitionSpec as P

OFFSETS = ((0, 0), (0, 1), (0, -1), (1, 0), (-1, 0), (1, -1), (-1, 1))
ANY = pl.BlockSpec(memory_space=pl.ANY)
VMEM = pl.BlockSpec(memory_space=pltpu.VMEM)


def remote(src, dst, send_sem, recv_sem, device_id):
    return pltpu.make_async_remote_copy(
        src_ref=src,
        dst_ref=dst,
        send_sem=send_sem,
        recv_sem=recv_sem,
        device_id=device_id,
        device_id_type=pl.DeviceIdType.MESH,
    )


def meet(whole_tile, whole_group):
    me, tiles = lax.axis_index("tile"), lax.axis_size("tile")
    chart, charts = lax.axis_index("diamond"), lax.axis_size("diamond")
    line, lines = lax.axis_index("tm"), lax.axis_size("tm")
    mine, size = line * charts + chart, lines * charts
    partners = [
        {"diamond": lax.rem(chart + turn, charts), "tile": lax.rem(me + step, tiles)}
        for turn in sorted({1, charts - 1})
        for step in range(tiles)
    ]
    steps = range(1, tiles) if whole_tile else sorted({1, tiles - 1})
    partners += [{"tile": lax.rem(me + step, tiles)} for step in steps]
    if whole_group:
        others = [lax.rem(mine + step, size) for step in range(1, size)]
        partners += [{"tm": one // charts, "diamond": lax.rem(one, charts)} for one in others]
    else:
        partners += [{"tm": lax.rem(line + step, lines)} for step in sorted({1, lines - 1})]
    barrier = pltpu.get_barrier_semaphore()
    for partner in partners:
        pl.semaphore_signal(
            barrier, inc=1, device_id=partner, device_id_type=pl.DeviceIdType.MESH
        )
    pl.semaphore_wait(barrier, len(partners))


def line_copies(axis, to_next, at_next, to_prev, at_prev, send, recv):
    me, size = lax.axis_index(axis), lax.axis_size(axis)
    up = remote(to_next, at_next, send.at[0], recv.at[0], {axis: lax.rem(me + 1, size)})
    down = remote(to_prev, at_prev, send.at[1], recv.at[1], {axis: lax.rem(me + size - 1, size)})

    def start():
        pl.when(me < size - 1)(up.start)
        pl.when(me > 0)(down.start)

    def wait():
        pl.when(me < size - 1)(up.wait_send)
        pl.when(me > 0)(down.wait_send)
        pl.when(me > 0)(up.wait_recv)
        pl.when(me < size - 1)(down.wait_recv)

    return start, wait


def seam_copies(strips, gathered, send, recv):
    me, tiles = lax.axis_index("tile"), lax.axis_size("tile")
    chart, charts = lax.axis_index("diamond"), lax.axis_size("diamond")
    sides = (lax.rem(chart + 1, charts), lax.rem(chart + charts - 1, charts))
    parts = (slice(0, 2),) if charts == 2 else (slice(0, 1), slice(1, 2))

    def copy(part, step, source, target):
        return remote(
            strips.at[parts[part]],
            gathered.at[source, parts[part]],
            send.at[part, step],
            recv.at[part, source],
            {"diamond": sides[part], "tile": target},
        )

    copies = [
        copy(part, step, me, lax.rem(me + step, tiles))
        for step in range(tiles)
        for part in range(len(parts))
    ]

    def start():
        for one in copies:
            one.start()

    def wait():
        for one in copies:
            one.wait_send()
        for part in range(len(parts)):
            for number in range(tiles):
                copy(part, 0, number, me).wait_recv()

    return start, wait


def first_exchange(
    strips, field, cotangent, gathered, above, below, before, after,
    seam_send, seam_recv, row_send, row_recv, frame_send, frame_recv,
):
    meet(False, False)
    rows, frames = field.shape[1], field.shape[0]
    parts = (
        seam_copies(strips, gathered, seam_send, seam_recv),
        line_copies("tile", field.at[:, rows - 1], above, field.at[:, 0], below, row_send, row_recv),
        line_copies(
            "tm", cotangent.at[frames - 1], before, cotangent.at[0], after, frame_send, frame_recv
        ),
    )
    for start, _ in parts:
        start()
    for _, wait in parts:
        wait()


def last_exchange(
    strips, up_row, down_row, terms, gathered, above, below, grad_hex, grad_time,
    seam_send, seam_recv, row_send, row_recv, sums,
    scattered, scatter_send, scatter_recv, group, group_send, group_recv, out_send, out_recv,
):
    meet(True, True)
    me, tiles = lax.axis_index("tile"), lax.axis_size("tile")
    charts, lines = lax.axis_size("diamond"), lax.axis_size("tm")
    mine = lax.axis_index("tm") * charts + lax.axis_index("diamond")
    size = lines * charts

    def tile_copy(src, dst, send, recv, step):
        return remote(src, dst, send.at[step], recv, {"tile": lax.rem(me + step, tiles)})

    first = [
        tile_copy(
            terms.at[:, lax.rem(me + step, tiles)], scattered.at[me], scatter_send,
            scatter_recv.at[me], step,
        )
        for step in range(1, tiles)
    ]
    for copy in first:
        copy.start()
    parts = (
        seam_copies(strips, gathered, seam_send, seam_recv),
        line_copies("tile", down_row, above, up_row, below, row_send, row_recv),
    )
    for start, _ in parts:
        start()
    total = terms[:, me]
    for step in range(1, tiles):
        other = lax.rem(me + step, tiles)
        tile_copy(
            terms.at[:, other], scattered.at[other], scatter_send, scatter_recv.at[other], step
        ).wait_recv()
        total = total + scattered[other]
    group[mine] = total
    second = []
    for step in range(1, size):
        other = lax.rem(mine + step, size)
        target = {"tm": other // charts, "diamond": lax.rem(other, charts)}
        copy = remote(
            group.at[mine], group.at[mine], group_send.at[step], group_recv.at[mine], target
        )
        copy.start()
        second.append(copy)
    for step in range(1, size):
        other = lax.rem(mine + step, size)
        target = {"tm": other // charts, "diamond": lax.rem(other, charts)}
        remote(
            group.at[other], group.at[other], group_send.at[step], group_recv.at[other], target
        ).wait_recv()
    total = group[0]
    for number in range(1, size):
        total = total + group[number]
    sums[me] = total
    third = [
        tile_copy(sums.at[me], sums.at[me], out_send, out_recv.at[me], step)
        for step in range(1, tiles)
    ]
    for copy in third:
        copy.start()
    for step in range(1, tiles):
        other = lax.rem(me + step, tiles)
        tile_copy(sums.at[other], sums.at[other], out_send, out_recv.at[other], step).wait_recv()
    channels = grad_hex.shape[1]
    pairs, _, span, _ = terms.shape
    taps = grad_hex.shape[0]
    for number in range(tiles):
        chunk = sums[number]
        rows = pl.ds(number * span, span)
        grad_hex[:pairs, rows] = chunk[..., :channels]
        grad_hex[pairs:, rows] = chunk[: taps - pairs, :, channels:]
        grad_time[:, rows] = chunk[taps - pairs :, :, channels:]
    for copy in first + second + third:
        copy.wait_send()
    for _, wait in parts:
        wait()


def exchange_start(strips, field, cotangent):
    frames, rows, channels, columns = field.shape
    tiles = lax.axis_size("tile")
    dma = pltpu.SemaphoreType.DMA
    kind = field.dtype
    line = jax.ShapeDtypeStruct((frames, channels, columns), kind)
    frame = jax.ShapeDtypeStruct((rows, channels, columns), kind)
    return pl.pallas_call(
        first_exchange,
        out_shape=(
            jax.ShapeDtypeStruct((tiles,) + strips.shape, kind), line, line, frame, frame,
        ),
        in_specs=[ANY] * 3,
        out_specs=(ANY,) * 5,
        scratch_shapes=[
            dma((2, tiles)), dma((2, tiles)), dma((2,)), dma((2,)), dma((2,)), dma((2,)),
        ],
        compiler_params=pltpu.CompilerParams(collective_id=0, has_side_effects=True),
        name="first_exchange",
    )(strips, field, cotangent)


def exchange_end(strips, up_row, down_row, terms):
    tiles = lax.axis_size("tile")
    size = lax.axis_size("tm") * lax.axis_size("diamond")
    dma = pltpu.SemaphoreType.DMA
    line = jax.ShapeDtypeStruct(up_row.shape, up_row.dtype)
    chunk = terms.shape[:1] + terms.shape[2:]
    channels = up_row.shape[1]
    return pl.pallas_call(
        last_exchange,
        out_shape=(
            jax.ShapeDtypeStruct((tiles,) + strips.shape, strips.dtype), line, line,
            jax.ShapeDtypeStruct((7, channels, channels), terms.dtype),
            jax.ShapeDtypeStruct((3, channels, channels), terms.dtype),
        ),
        in_specs=[ANY, ANY, ANY, VMEM],
        out_specs=(ANY, ANY, ANY, VMEM, VMEM),
        scratch_shapes=[
            dma((2, tiles)), dma((2, tiles)), dma((2,)), dma((2,)),
            pltpu.VMEM((tiles,) + chunk, terms.dtype),
            pltpu.VMEM((tiles,) + chunk, terms.dtype), dma((tiles,)), dma((tiles,)),
            pltpu.VMEM((size,) + chunk, terms.dtype), dma((size,)), dma((size,)),
            dma((tiles,)), dma((tiles,)),
        ],
        compiler_params=pltpu.CompilerParams(collective_id=1, has_side_effects=True),
        name="last_exchange",
    )(strips, up_row, down_row, terms)


def silu_slope(hidden):
    sigmoid = jax.nn.sigmoid(hidden)
    return sigmoid * (1.0 + hidden * (1.0 - sigmoid))


def local_math(padded, framed, hex_weight, time_weight, frames, tile_rows, channels, columns):
    row_major = Layout(major_to_minor=(0, 1, 2, 3))
    padded = with_layout_constraint(padded, row_major)
    hidden = jnp.zeros((frames, tile_rows, channels, columns), jnp.float32)
    windows = [
        padded[:, 1 + a : 1 + a + tile_rows, :, 1 + b : 1 + b + columns] for a, b in OFFSETS
    ]
    for number in range(7):
        hidden = hidden + jnp.einsum(
            "frcx,cd->frdx", windows[number], hex_weight[number],
            preferred_element_type=jnp.float32,
        )
    active = jax.nn.silu(hidden).astype(jnp.bfloat16)
    grad_act = jnp.zeros((frames, tile_rows, channels, columns), jnp.float32)
    time_terms = []
    for number in range(3):
        shifted = framed[2 - number : 2 - number + frames]
        grad_act = grad_act + jnp.einsum(
            "frdx,cd->frcx", shifted, time_weight[number], preferred_element_type=jnp.float32
        )
        time_terms.append(
            jnp.einsum("frcx,frdx->cd", active, shifted, preferred_element_type=jnp.float32)
        )
    grad_wide = (grad_act * silu_slope(hidden)).astype(jnp.bfloat16)
    grad_wide = with_layout_constraint(grad_wide, row_major)
    hex_terms = [
        jnp.einsum("frcx,frdx->cd", window, grad_wide, preferred_element_type=jnp.float32)
        for window in windows
    ]
    spread = up_row = down_row = None
    for number, (a, b) in enumerate(OFFSETS):
        term = jnp.einsum(
            "frdx,cd->frcx", grad_wide, hex_weight[number], preferred_element_type=jnp.float32
        )
        if b == 1:
            term = jnp.pad(term[..., :-1], ((0, 0), (0, 0), (0, 0), (1, 0)))
        if b == -1:
            term = jnp.pad(term[..., 1:], ((0, 0), (0, 0), (0, 0), (0, 1)))
        if a == 1:
            down_row = term[:, -1] if down_row is None else down_row + term[:, -1]
            term = jnp.pad(term[:, :-1], ((0, 0), (1, 0), (0, 0), (0, 0)))
        if a == -1:
            up_row = term[:, 0] if up_row is None else up_row + term[:, 0]
            term = jnp.pad(term[:, 1:], ((0, 0), (0, 1), (0, 0), (0, 0)))
        spread = term if spread is None else spread + term
    edges = up_row.astype(jnp.bfloat16), down_row.astype(jnp.bfloat16)
    seams = seam_columns(grad_wide)
    sides = []
    for side, b in ((0, 1), (1, -1)):
        seam = None
        for number, (a, _) in enumerate(OFFSETS):
            if OFFSETS[number][1] == b:
                term = jnp.einsum(
                    "frd,cd->frc", seams[side], hex_weight[number],
                    preferred_element_type=jnp.float32,
                )
                term = jnp.pad(term, ((0, 0), (1 + a, 1 - a), (0, 0)))
                seam = term if seam is None else seam + term
        sides.append(seam)
    pairs = zip(hex_terms[:5], hex_terms[5:] + time_terms)
    terms = jnp.stack([jnp.concatenate(pair, axis=-1) for pair in pairs])
    return spread, edges, jnp.stack(sides).astype(jnp.bfloat16), terms


def seam_columns(block):
    return jnp.stack([block[..., block.shape[-1] - 1], block[..., 0]])


def shards(activations, upstream, hex_weight, time_weight, left_map, right_map):
    field = activations[:, 0]
    row_major = Layout(major_to_minor=(0, 1, 2, 3))
    cotangent = with_layout_constraint(upstream[:, 0], row_major)
    frames, tile_rows, channels, columns = field.shape
    chart, charts = lax.axis_index("diamond"), lax.axis_size("diamond")
    tile, tiles = lax.axis_index("tile"), lax.axis_size("tile")
    line, lines = lax.axis_index("tm"), lax.axis_size("tm")
    first_row = tile * tile_rows
    wide = tile_rows + 2
    strips = seam_columns(field).reshape(2, frames * tile_rows, channels)
    gathered, above, below, before, after = exchange_start(strips, field, cotangent)
    above = jnp.where(tile > 0, above, 0)
    below = jnp.where(tile < tiles - 1, below, 0)
    before = jnp.where(line > 0, before, 0)
    after = jnp.where(line < lines - 1, after, 0)

    def chart_rows(table, number):
        own = lax.dynamic_slice(table, (number, 0), (1, table.shape[1]))[0]
        return jnp.pad(own, (1, 1), constant_values=-1)

    every = jnp.arange(tiles * tile_rows)

    def ghost(strip, table):
        own = lax.dynamic_slice(chart_rows(table, chart), (first_row,), (wide,))
        pick = (own[:, None] == every[None, :]).astype(jnp.bfloat16)
        pick = pick.reshape(wide, tiles, tile_rows)
        strip = strip.reshape(tiles, frames, tile_rows, channels)
        return jnp.einsum("wtr,tfrc->fwc", pick, strip, preferred_element_type=jnp.float32).astype(
            jnp.bfloat16
        )

    ghost_left = ghost(gathered[:, 0], left_map)
    ghost_right = ghost(gathered[:, 1], right_map)
    rows = jnp.concatenate([above[:, None], field, below[:, None]], axis=1)
    padded = jnp.concatenate([ghost_left[..., None], rows, ghost_right[..., None]], axis=-1)
    framed = jnp.concatenate([before[None], cotangent, after[None]], axis=0)
    spread, edges, seams, terms = local_math(
        padded, framed, hex_weight, time_weight, frames, tile_rows, channels, columns
    )
    strips = seams.reshape(2, frames * wide, channels)
    gathered, above, below, grad_hex, grad_time = exchange_end(
        strips, *edges, terms.reshape(terms.shape[0], tiles, channels // tiles, 2 * channels)
    )
    row = jnp.arange(tile_rows)[:, None, None]
    total = cotangent.astype(jnp.float32) + spread
    total = total + jnp.where(
        (row == 0) & (tile > 0), above[:, None].astype(jnp.float32), 0.0
    )
    total = total + jnp.where(
        (row == tile_rows - 1) & (tile < tiles - 1), below[:, None].astype(jnp.float32), 0.0
    )
    own_rows = first_row + jnp.arange(tile_rows)

    def landing(strip, table, number):
        target = chart_rows(table, number)
        inner = target[1:-1].reshape(tiles, tile_rows)
        prior = target[:-2].reshape(tiles, tile_rows)[:, :1]
        later = target[2:].reshape(tiles, tile_rows)[:, -1:]
        target = jnp.concatenate([prior, inner, later], axis=1)
        pick = (own_rows[:, None, None] == target[None]).astype(jnp.bfloat16)
        strip = strip.reshape(tiles, frames, wide, channels)
        return jnp.einsum("rtw,tfwc->frc", pick, strip, preferred_element_type=jnp.float32)

    into_first = landing(gathered[:, 0], right_map, lax.rem(chart + charts - 1, charts))
    into_last = landing(gathered[:, 1], left_map, lax.rem(chart + 1, charts))
    column = jnp.arange(columns)
    total = total + jnp.where(column == 0, into_first[..., None], 0.0)
    total = total + jnp.where(column == columns - 1, into_last[..., None], 0.0)
    total = with_layout_constraint(total.astype(jnp.bfloat16), row_major)
    return total[:, None], grad_hex, grad_time


def solution(mesh):
    whole = P("tm", "diamond", "tile", None, None)
    return jax.shard_map(
        shards,
        mesh=mesh,
        in_specs=(whole, whole, P(), P(), P(), P()),
        out_specs=(whole, P(), P()),
        check_vma=False,
    )
```

```python
import jax
import jax.numpy as jnp
from jax import lax
from jax.experimental import pallas as pl
from jax.experimental.pallas import tpu as pltpu
from jax.sharding import PartitionSpec as P

OFFSETS = ((0, 0), (0, 1), (0, -1), (1, 0), (-1, 0), (1, -1), (-1, 1))
ANY = pl.BlockSpec(memory_space=pl.ANY)
VMEM = pl.BlockSpec(memory_space=pltpu.VMEM)


def remote(src, dst, send_sem, recv_sem, device_id):
    return pltpu.make_async_remote_copy(
        src_ref=src,
        dst_ref=dst,
        send_sem=send_sem,
        recv_sem=recv_sem,
        device_id=device_id,
        device_id_type=pl.DeviceIdType.MESH,
    )


def meet(whole_tile, whole_group):
    me, tiles = lax.axis_index("tile"), lax.axis_size("tile")
    chart, charts = lax.axis_index("diamond"), lax.axis_size("diamond")
    line, lines = lax.axis_index("tm"), lax.axis_size("tm")
    mine, size = line * charts + chart, lines * charts
    partners = [
        {"diamond": lax.rem(chart + turn, charts), "tile": lax.rem(me + step, tiles)}
        for turn in sorted({1, charts - 1})
        for step in range(tiles)
    ]
    steps = range(1, tiles) if whole_tile else sorted({1, tiles - 1})
    partners += [{"tile": lax.rem(me + step, tiles)} for step in steps]
    if whole_group:
        others = [lax.rem(mine + step, size) for step in range(1, size)]
        partners += [{"tm": one // charts, "diamond": lax.rem(one, charts)} for one in others]
    else:
        partners += [{"tm": lax.rem(line + step, lines)} for step in sorted({1, lines - 1})]
    barrier = pltpu.get_barrier_semaphore()
    for partner in partners:
        pl.semaphore_signal(
            barrier, inc=1, device_id=partner, device_id_type=pl.DeviceIdType.MESH
        )
    pl.semaphore_wait(barrier, len(partners))


def line_copies(axis, to_next, at_next, to_prev, at_prev, send, recv):
    me, size = lax.axis_index(axis), lax.axis_size(axis)
    up = remote(to_next, at_next, send.at[0], recv.at[0], {axis: lax.rem(me + 1, size)})
    down = remote(to_prev, at_prev, send.at[1], recv.at[1], {axis: lax.rem(me + size - 1, size)})

    def start():
        pl.when(me < size - 1)(up.start)
        pl.when(me > 0)(down.start)

    def wait():
        pl.when(me < size - 1)(up.wait_send)
        pl.when(me > 0)(down.wait_send)
        pl.when(me > 0)(up.wait_recv)
        pl.when(me < size - 1)(down.wait_recv)

    return start, wait


def seam_copies(strips, gathered, send, recv):
    me, tiles = lax.axis_index("tile"), lax.axis_size("tile")
    chart, charts = lax.axis_index("diamond"), lax.axis_size("diamond")
    sides = (lax.rem(chart + 1, charts), lax.rem(chart + charts - 1, charts))
    parts = (slice(0, 2),) if charts == 2 else (slice(0, 1), slice(1, 2))

    def copy(part, step, source, target):
        return remote(
            strips.at[parts[part]],
            gathered.at[source, parts[part]],
            send.at[part, step],
            recv.at[part, source],
            {"diamond": sides[part], "tile": target},
        )

    copies = [
        copy(part, step, me, lax.rem(me + step, tiles))
        for step in range(tiles)
        for part in range(len(parts))
    ]

    def start():
        for one in copies:
            one.start()

    def wait():
        for one in copies:
            one.wait_send()
        for part in range(len(parts)):
            for number in range(tiles):
                copy(part, 0, number, me).wait_recv()

    return start, wait


def first_exchange(
    strips, field, cotangent, gathered, above, below, before, after,
    seam_send, seam_recv, row_send, row_recv, frame_send, frame_recv,
):
    meet(False, False)
    rows, frames = field.shape[1], field.shape[0]
    parts = (
        seam_copies(strips, gathered, seam_send, seam_recv),
        line_copies("tile", field.at[:, rows - 1], above, field.at[:, 0], below, row_send, row_recv),
        line_copies(
            "tm", cotangent.at[frames - 1], before, cotangent.at[0], after, frame_send, frame_recv
        ),
    )
    for start, _ in parts:
        start()
    for _, wait in parts:
        wait()


def last_exchange(
    strips, up_row, down_row, terms, gathered, above, below, grad_hex, grad_time,
    seam_send, seam_recv, row_send, row_recv, sums,
    scattered, scatter_send, scatter_recv, group, group_send, group_recv, out_send, out_recv,
):
    meet(True, True)
    me, tiles = lax.axis_index("tile"), lax.axis_size("tile")
    charts, lines = lax.axis_size("diamond"), lax.axis_size("tm")
    mine = lax.axis_index("tm") * charts + lax.axis_index("diamond")
    size = lines * charts

    def tile_copy(src, dst, send, recv, step):
        return remote(src, dst, send.at[step], recv, {"tile": lax.rem(me + step, tiles)})

    first = [
        tile_copy(
            terms.at[:, lax.rem(me + step, tiles)], scattered.at[me], scatter_send,
            scatter_recv.at[me], step,
        )
        for step in range(1, tiles)
    ]
    for copy in first:
        copy.start()
    parts = (
        seam_copies(strips, gathered, seam_send, seam_recv),
        line_copies("tile", down_row, above, up_row, below, row_send, row_recv),
    )
    for start, _ in parts:
        start()
    total = terms[:, me]
    for step in range(1, tiles):
        other = lax.rem(me + step, tiles)
        tile_copy(
            terms.at[:, other], scattered.at[other], scatter_send, scatter_recv.at[other], step
        ).wait_recv()
        total = total + scattered[other]
    group[mine] = total
    second = []
    for step in range(1, size):
        other = lax.rem(mine + step, size)
        target = {"tm": other // charts, "diamond": lax.rem(other, charts)}
        copy = remote(
            group.at[mine], group.at[mine], group_send.at[step], group_recv.at[mine], target
        )
        copy.start()
        second.append(copy)
    for step in range(1, size):
        other = lax.rem(mine + step, size)
        target = {"tm": other // charts, "diamond": lax.rem(other, charts)}
        remote(
            group.at[other], group.at[other], group_send.at[step], group_recv.at[other], target
        ).wait_recv()
    total = group[0]
    for number in range(1, size):
        total = total + group[number]
    sums[me] = total
    third = [
        tile_copy(sums.at[me], sums.at[me], out_send, out_recv.at[me], step)
        for step in range(1, tiles)
    ]
    for copy in third:
        copy.start()
    for step in range(1, tiles):
        other = lax.rem(me + step, tiles)
        tile_copy(sums.at[other], sums.at[other], out_send, out_recv.at[other], step).wait_recv()
    channels = grad_hex.shape[1]
    pairs, _, span, _ = terms.shape
    taps = grad_hex.shape[0]
    for number in range(tiles):
        chunk = sums[number]
        rows = pl.ds(number * span, span)
        grad_hex[:pairs, rows] = chunk[..., :channels]
        grad_hex[pairs:, rows] = chunk[: taps - pairs, :, channels:]
        grad_time[:, rows] = chunk[taps - pairs :, :, channels:]
    for copy in first + second + third:
        copy.wait_send()
    for _, wait in parts:
        wait()


def exchange_start(strips, field, cotangent):
    frames, rows, channels, columns = field.shape
    tiles = lax.axis_size("tile")
    dma = pltpu.SemaphoreType.DMA
    kind = field.dtype
    line = jax.ShapeDtypeStruct((frames, channels, columns), kind)
    frame = jax.ShapeDtypeStruct((rows, channels, columns), kind)
    return pl.pallas_call(
        first_exchange,
        out_shape=(
            jax.ShapeDtypeStruct((tiles,) + strips.shape, kind), line, line, frame, frame,
        ),
        in_specs=[ANY] * 3,
        out_specs=(ANY,) * 5,
        scratch_shapes=[
            dma((2, tiles)), dma((2, tiles)), dma((2,)), dma((2,)), dma((2,)), dma((2,)),
        ],
        compiler_params=pltpu.CompilerParams(collective_id=0, has_side_effects=True),
        name="first_exchange",
    )(strips, field, cotangent)


def exchange_end(strips, up_row, down_row, terms):
    tiles = lax.axis_size("tile")
    size = lax.axis_size("tm") * lax.axis_size("diamond")
    dma = pltpu.SemaphoreType.DMA
    line = jax.ShapeDtypeStruct(up_row.shape, up_row.dtype)
    chunk = terms.shape[:1] + terms.shape[2:]
    channels = up_row.shape[1]
    return pl.pallas_call(
        last_exchange,
        out_shape=(
            jax.ShapeDtypeStruct((tiles,) + strips.shape, strips.dtype), line, line,
            jax.ShapeDtypeStruct((7, channels, channels), terms.dtype),
            jax.ShapeDtypeStruct((3, channels, channels), terms.dtype),
        ),
        in_specs=[ANY, ANY, ANY, VMEM],
        out_specs=(ANY, ANY, ANY, VMEM, VMEM),
        scratch_shapes=[
            dma((2, tiles)), dma((2, tiles)), dma((2,)), dma((2,)),
            pltpu.VMEM((tiles,) + chunk, terms.dtype),
            pltpu.VMEM((tiles,) + chunk, terms.dtype), dma((tiles,)), dma((tiles,)),
            pltpu.VMEM((size,) + chunk, terms.dtype), dma((size,)), dma((size,)),
            dma((tiles,)), dma((tiles,)),
        ],
        compiler_params=pltpu.CompilerParams(collective_id=1, has_side_effects=True),
        name="last_exchange",
    )(strips, up_row, down_row, terms)


def silu_slope(hidden):
    sigmoid = jax.nn.sigmoid(hidden)
    return sigmoid * (1.0 + hidden * (1.0 - sigmoid))


def local_math(padded, framed, hex_weight, time_weight, frames, tile_rows, channels, columns):
    hidden = jnp.zeros((frames, tile_rows, channels, columns), jnp.float32)
    windows = [
        padded[:, 1 + a : 1 + a + tile_rows, :, 1 + b : 1 + b + columns] for a, b in OFFSETS
    ]
    for number in range(7):
        hidden = hidden + jnp.einsum(
            "frcx,cd->frdx", windows[number], hex_weight[number],
            preferred_element_type=jnp.float32,
        )
    active = jax.nn.silu(hidden).astype(jnp.bfloat16)
    grad_act = jnp.zeros((frames, tile_rows, channels, columns), jnp.float32)
    time_terms = []
    for number in range(3):
        shifted = framed[2 - number : 2 - number + frames]
        grad_act = grad_act + jnp.einsum(
            "frdx,cd->frcx", shifted, time_weight[number], preferred_element_type=jnp.float32
        )
        time_terms.append(
            jnp.einsum("frcx,frdx->cd", active, shifted, preferred_element_type=jnp.float32)
        )
    grad_wide = (grad_act * silu_slope(hidden)).astype(jnp.bfloat16)
    hex_terms = [
        jnp.einsum("frcx,frdx->cd", window, grad_wide, preferred_element_type=jnp.float32)
        for window in windows
    ]
    spread = None
    for number, (a, b) in enumerate(OFFSETS):
        term = jnp.einsum(
            "frdx,cd->frcx", grad_wide, hex_weight[number], preferred_element_type=jnp.float32
        )
        if b == 1:
            term = jnp.pad(term[..., :-1], ((0, 0), (0, 0), (0, 0), (1, 0)))
        if b == -1:
            term = jnp.pad(term[..., 1:], ((0, 0), (0, 0), (0, 0), (0, 1)))
        term = jnp.pad(term, ((0, 0), (1 + a, 1 - a), (0, 0), (0, 0)))
        spread = term if spread is None else spread + term
    seams = seam_columns(grad_wide)
    sides = []
    for side, b in ((0, 1), (1, -1)):
        seam = None
        for number, (a, _) in enumerate(OFFSETS):
            if OFFSETS[number][1] == b:
                term = jnp.einsum(
                    "frd,cd->frc", seams[side], hex_weight[number],
                    preferred_element_type=jnp.float32,
                )
                term = jnp.pad(term, ((0, 0), (1 + a, 1 - a), (0, 0)))
                seam = term if seam is None else seam + term
        sides.append(seam)
    pairs = zip(hex_terms[:5], hex_terms[5:] + time_terms)
    terms = jnp.stack([jnp.concatenate(pair, axis=-1) for pair in pairs])
    return spread, jnp.stack(sides).astype(jnp.bfloat16), terms


def seam_columns(block):
    return jnp.stack([block[..., block.shape[-1] - 1], block[..., 0]])


def shards(activations, upstream, hex_weight, time_weight, left_map, right_map):
    field = activations[:, 0]
    cotangent = upstream[:, 0]
    frames, tile_rows, channels, columns = field.shape
    chart, charts = lax.axis_index("diamond"), lax.axis_size("diamond")
    tile, tiles = lax.axis_index("tile"), lax.axis_size("tile")
    line, lines = lax.axis_index("tm"), lax.axis_size("tm")
    first_row = tile * tile_rows
    wide = tile_rows + 2
    strips = seam_columns(field).reshape(2, frames * tile_rows, channels)
    gathered, above, below, before, after = exchange_start(strips, field, cotangent)
    above = jnp.where(tile > 0, above, 0)
    below = jnp.where(tile < tiles - 1, below, 0)
    before = jnp.where(line > 0, before, 0)
    after = jnp.where(line < lines - 1, after, 0)

    def chart_rows(table, number):
        own = lax.dynamic_slice(table, (number, 0), (1, table.shape[1]))[0]
        return jnp.pad(own, (1, 1), constant_values=-1)

    every = jnp.arange(tiles * tile_rows)

    def ghost(strip, table):
        own = lax.dynamic_slice(chart_rows(table, chart), (first_row,), (wide,))
        pick = (own[:, None] == every[None, :]).astype(jnp.bfloat16)
        pick = pick.reshape(wide, tiles, tile_rows)
        strip = strip.reshape(tiles, frames, tile_rows, channels)
        return jnp.einsum("wtr,tfrc->fwc", pick, strip, preferred_element_type=jnp.float32).astype(
            jnp.bfloat16
        )

    ghost_left = ghost(gathered[:, 0], left_map)
    ghost_right = ghost(gathered[:, 1], right_map)
    rows = jnp.concatenate([above[:, None], field, below[:, None]], axis=1)
    padded = jnp.concatenate([ghost_left[..., None], rows, ghost_right[..., None]], axis=-1)
    framed = jnp.concatenate([before[None], cotangent, after[None]], axis=0)
    spread, seams, terms = local_math(
        padded, framed, hex_weight, time_weight, frames, tile_rows, channels, columns
    )
    strips = seams.reshape(2, frames * wide, channels)
    gathered, above, below, grad_hex, grad_time = exchange_end(
        strips, spread[:, 0].astype(jnp.bfloat16), spread[:, wide - 1].astype(jnp.bfloat16),
        terms.reshape(terms.shape[0], tiles, channels // tiles, 2 * channels),
    )
    total = cotangent.astype(jnp.float32) + spread[:, 1 : tile_rows + 1]
    above = jnp.where(tile > 0, above, 0).astype(jnp.float32)
    below = jnp.where(tile < tiles - 1, below, 0).astype(jnp.float32)
    total = total + jnp.pad(above[:, None], ((0, 0), (0, tile_rows - 1), (0, 0), (0, 0)))
    total = total + jnp.pad(below[:, None], ((0, 0), (tile_rows - 1, 0), (0, 0), (0, 0)))
    own_rows = first_row + jnp.arange(tile_rows)

    def landing(strip, table, number):
        target = chart_rows(table, number)
        inner = target[1:-1].reshape(tiles, tile_rows)
        prior = target[:-2].reshape(tiles, tile_rows)[:, :1]
        later = target[2:].reshape(tiles, tile_rows)[:, -1:]
        target = jnp.concatenate([prior, inner, later], axis=1)
        pick = (own_rows[:, None, None] == target[None]).astype(jnp.bfloat16)
        strip = strip.reshape(tiles, frames, wide, channels)
        return jnp.einsum("rtw,tfwc->frc", pick, strip, preferred_element_type=jnp.float32)

    into_first = landing(gathered[:, 0], right_map, lax.rem(chart + charts - 1, charts))
    into_last = landing(gathered[:, 1], left_map, lax.rem(chart + 1, charts))
    column = jnp.arange(columns)
    total = total + jnp.where(column == 0, into_first[..., None], 0.0)
    total = total + jnp.where(column == columns - 1, into_last[..., None], 0.0)
    return total.astype(jnp.bfloat16)[:, None], grad_hex, grad_time


def solution(mesh):
    whole = P("tm", "diamond", "tile", None, None)
    return jax.shard_map(
        shards,
        mesh=mesh,
        in_specs=(whole, whole, P(), P(), P(), P()),
        out_specs=(whole, P(), P()),
        check_vma=False,
    )
```

```python
import jax
import jax.numpy as jnp
from jax import lax
from jax.experimental import pallas as pl
from jax.experimental.pallas import tpu as pltpu
from jax.sharding import PartitionSpec as P

OFFSETS = ((0, 0), (0, 1), (0, -1), (1, 0), (-1, 0), (1, -1), (-1, 1))
ANY = pl.BlockSpec(memory_space=pl.ANY)
VMEM = pl.BlockSpec(memory_space=pltpu.VMEM)


def remote(src, dst, send_sem, recv_sem, device_id):
    return pltpu.make_async_remote_copy(
        src_ref=src,
        dst_ref=dst,
        send_sem=send_sem,
        recv_sem=recv_sem,
        device_id=device_id,
        device_id_type=pl.DeviceIdType.MESH,
    )


def meet(whole_tile, whole_group):
    me, tiles = lax.axis_index("tile"), lax.axis_size("tile")
    chart, charts = lax.axis_index("diamond"), lax.axis_size("diamond")
    line, lines = lax.axis_index("tm"), lax.axis_size("tm")
    mine, size = line * charts + chart, lines * charts
    partners = [
        {"diamond": lax.rem(chart + turn, charts), "tile": lax.rem(me + step, tiles)}
        for turn in sorted({1, charts - 1})
        for step in range(tiles)
    ]
    steps = range(1, tiles) if whole_tile else sorted({1, tiles - 1})
    partners += [{"tile": lax.rem(me + step, tiles)} for step in steps]
    if whole_group:
        others = [lax.rem(mine + step, size) for step in range(1, size)]
        partners += [{"tm": one // charts, "diamond": lax.rem(one, charts)} for one in others]
    else:
        partners += [{"tm": lax.rem(line + step, lines)} for step in sorted({1, lines - 1})]
    barrier = pltpu.get_barrier_semaphore()
    for partner in partners:
        pl.semaphore_signal(
            barrier, inc=1, device_id=partner, device_id_type=pl.DeviceIdType.MESH
        )
    pl.semaphore_wait(barrier, len(partners))


def line_copies(axis, to_next, at_next, to_prev, at_prev, send, recv):
    me, size = lax.axis_index(axis), lax.axis_size(axis)
    up = remote(to_next, at_next, send.at[0], recv.at[0], {axis: lax.rem(me + 1, size)})
    down = remote(to_prev, at_prev, send.at[1], recv.at[1], {axis: lax.rem(me + size - 1, size)})

    def start():
        pl.when(me < size - 1)(up.start)
        pl.when(me > 0)(down.start)

    def wait():
        pl.when(me < size - 1)(up.wait_send)
        pl.when(me > 0)(down.wait_send)
        pl.when(me > 0)(up.wait_recv)
        pl.when(me < size - 1)(down.wait_recv)

    return start, wait


def seam_copies(strips, gathered, send, recv):
    me, tiles = lax.axis_index("tile"), lax.axis_size("tile")
    chart, charts = lax.axis_index("diamond"), lax.axis_size("diamond")
    sides = (lax.rem(chart + 1, charts), lax.rem(chart + charts - 1, charts))
    parts = (slice(0, 2),) if charts == 2 else (slice(0, 1), slice(1, 2))

    def copy(part, step, source, target):
        return remote(
            strips.at[parts[part]],
            gathered.at[source, parts[part]],
            send.at[part, step],
            recv.at[part, source],
            {"diamond": sides[part], "tile": target},
        )

    copies = [
        copy(part, step, me, lax.rem(me + step, tiles))
        for step in range(tiles)
        for part in range(len(parts))
    ]

    def start():
        for one in copies:
            one.start()

    def wait():
        for one in copies:
            one.wait_send()
        for part in range(len(parts)):
            for number in range(tiles):
                copy(part, 0, number, me).wait_recv()

    return start, wait


def first_exchange(
    strips, field, cotangent, gathered, above, below, before, after,
    seam_send, seam_recv, row_send, row_recv, frame_send, frame_recv,
):
    meet(False, False)
    rows, frames = field.shape[1], field.shape[0]
    parts = (
        line_copies(
            "tm", cotangent.at[frames - 1], before, cotangent.at[0], after, frame_send, frame_recv
        ),
        line_copies("tile", field.at[:, rows - 1], above, field.at[:, 0], below, row_send, row_recv),
        seam_copies(strips, gathered, seam_send, seam_recv),
    )
    for start, _ in parts:
        start()
    for _, wait in parts:
        wait()


def last_exchange(
    strips, up_row, down_row, terms, gathered, above, below, grad_hex, grad_time,
    seam_send, seam_recv, row_send, row_recv, sums,
    scattered, scatter_send, scatter_recv, group, group_send, group_recv, out_send, out_recv,
):
    meet(True, True)
    me, tiles = lax.axis_index("tile"), lax.axis_size("tile")
    charts, lines = lax.axis_size("diamond"), lax.axis_size("tm")
    mine = lax.axis_index("tm") * charts + lax.axis_index("diamond")
    size = lines * charts

    def tile_copy(src, dst, send, recv, step):
        return remote(src, dst, send.at[step], recv, {"tile": lax.rem(me + step, tiles)})

    first = [
        tile_copy(
            terms.at[:, lax.rem(me + step, tiles)], scattered.at[me], scatter_send,
            scatter_recv.at[me], step,
        )
        for step in range(1, tiles)
    ]
    for copy in first:
        copy.start()
    parts = (
        seam_copies(strips, gathered, seam_send, seam_recv),
        line_copies("tile", down_row, above, up_row, below, row_send, row_recv),
    )
    total = terms[:, me]
    for step in range(1, tiles):
        other = lax.rem(me + step, tiles)
        tile_copy(
            terms.at[:, other], scattered.at[other], scatter_send, scatter_recv.at[other], step
        ).wait_recv()
        total = total + scattered[other]
    group[mine] = total
    second = []
    for step in range(1, size):
        other = lax.rem(mine + step, size)
        target = {"tm": other // charts, "diamond": lax.rem(other, charts)}
        copy = remote(
            group.at[mine], group.at[mine], group_send.at[step], group_recv.at[mine], target
        )
        copy.start()
        second.append(copy)
    for start, _ in parts:
        start()
    for step in range(1, size):
        other = lax.rem(mine + step, size)
        target = {"tm": other // charts, "diamond": lax.rem(other, charts)}
        remote(
            group.at[other], group.at[other], group_send.at[step], group_recv.at[other], target
        ).wait_recv()
    total = group[0]
    for number in range(1, size):
        total = total + group[number]
    sums[me] = total
    third = [
        tile_copy(sums.at[me], sums.at[me], out_send, out_recv.at[me], step)
        for step in range(1, tiles)
    ]
    for copy in third:
        copy.start()
    for step in range(1, tiles):
        other = lax.rem(me + step, tiles)
        tile_copy(sums.at[other], sums.at[other], out_send, out_recv.at[other], step).wait_recv()
    channels = grad_hex.shape[1]
    pairs, _, span, _ = terms.shape
    taps = grad_hex.shape[0]
    for number in range(tiles):
        chunk = sums[number]
        rows = pl.ds(number * span, span)
        grad_hex[:pairs, rows] = chunk[..., :channels]
        grad_hex[pairs:, rows] = chunk[: taps - pairs, :, channels:]
        grad_time[:, rows] = chunk[taps - pairs :, :, channels:]
    for copy in first + second + third:
        copy.wait_send()
    for _, wait in parts:
        wait()


def exchange_start(strips, field, cotangent):
    frames, rows, channels, columns = field.shape
    tiles = lax.axis_size("tile")
    dma = pltpu.SemaphoreType.DMA
    kind = field.dtype
    line = jax.ShapeDtypeStruct((frames, channels, columns), kind)
    frame = jax.ShapeDtypeStruct((rows, channels, columns), kind)
    return pl.pallas_call(
        first_exchange,
        out_shape=(
            jax.ShapeDtypeStruct((tiles,) + strips.shape, kind), line, line, frame, frame,
        ),
        in_specs=[ANY] * 3,
        out_specs=(ANY,) * 5,
        scratch_shapes=[
            dma((2, tiles)), dma((2, tiles)), dma((2,)), dma((2,)), dma((2,)), dma((2,)),
        ],
        compiler_params=pltpu.CompilerParams(collective_id=0, has_side_effects=True),
        name="first_exchange",
    )(strips, field, cotangent)


def exchange_end(strips, up_row, down_row, terms):
    tiles = lax.axis_size("tile")
    size = lax.axis_size("tm") * lax.axis_size("diamond")
    dma = pltpu.SemaphoreType.DMA
    line = jax.ShapeDtypeStruct(up_row.shape, up_row.dtype)
    chunk = terms.shape[:1] + terms.shape[2:]
    channels = up_row.shape[1]
    return pl.pallas_call(
        last_exchange,
        out_shape=(
            jax.ShapeDtypeStruct((tiles,) + strips.shape, strips.dtype), line, line,
            jax.ShapeDtypeStruct((7, channels, channels), terms.dtype),
            jax.ShapeDtypeStruct((3, channels, channels), terms.dtype),
        ),
        in_specs=[ANY, ANY, ANY, VMEM],
        out_specs=(ANY, ANY, ANY, VMEM, VMEM),
        scratch_shapes=[
            dma((2, tiles)), dma((2, tiles)), dma((2,)), dma((2,)),
            pltpu.VMEM((tiles,) + chunk, terms.dtype),
            pltpu.VMEM((tiles,) + chunk, terms.dtype), dma((tiles,)), dma((tiles,)),
            pltpu.VMEM((size,) + chunk, terms.dtype), dma((size,)), dma((size,)),
            dma((tiles,)), dma((tiles,)),
        ],
        compiler_params=pltpu.CompilerParams(collective_id=1, has_side_effects=True),
        name="last_exchange",
    )(strips, up_row, down_row, terms)


def silu_slope(hidden):
    sigmoid = jax.nn.sigmoid(hidden)
    return sigmoid * (1.0 + hidden * (1.0 - sigmoid))


def local_math(padded, framed, hex_weight, time_weight, frames, tile_rows, channels, columns):
    hidden = jnp.zeros((frames, tile_rows, channels, columns), jnp.float32)
    windows = [
        padded[:, 1 + a : 1 + a + tile_rows, :, 1 + b : 1 + b + columns] for a, b in OFFSETS
    ]
    for number in range(7):
        hidden = hidden + jnp.einsum(
            "frcx,cd->frdx", windows[number], hex_weight[number],
            preferred_element_type=jnp.float32,
        )
    active = jax.nn.silu(hidden).astype(jnp.bfloat16)
    grad_act = jnp.zeros((frames, tile_rows, channels, columns), jnp.float32)
    time_terms = []
    for number in range(3):
        shifted = framed[2 - number : 2 - number + frames]
        grad_act = grad_act + jnp.einsum(
            "frdx,cd->frcx", shifted, time_weight[number], preferred_element_type=jnp.float32
        )
        time_terms.append(
            jnp.einsum("frcx,frdx->cd", active, shifted, preferred_element_type=jnp.float32)
        )
    grad_wide = (grad_act * silu_slope(hidden)).astype(jnp.bfloat16)
    hex_terms = [
        jnp.einsum("frcx,frdx->cd", window, grad_wide, preferred_element_type=jnp.float32)
        for window in windows
    ]
    spread = None
    for number, (a, b) in enumerate(OFFSETS):
        term = jnp.einsum(
            "frdx,cd->frcx", grad_wide, hex_weight[number], preferred_element_type=jnp.float32
        )
        if b == 1:
            term = jnp.pad(term[..., :-1], ((0, 0), (0, 0), (0, 0), (1, 0)))
        if b == -1:
            term = jnp.pad(term[..., 1:], ((0, 0), (0, 0), (0, 0), (0, 1)))
        term = jnp.pad(term, ((0, 0), (1 + a, 1 - a), (0, 0), (0, 0)))
        spread = term if spread is None else spread + term
    seams = seam_columns(grad_wide)
    sides = []
    for side, b in ((0, 1), (1, -1)):
        seam = None
        for number, (a, _) in enumerate(OFFSETS):
            if OFFSETS[number][1] == b:
                term = jnp.einsum(
                    "frd,cd->frc", seams[side], hex_weight[number],
                    preferred_element_type=jnp.float32,
                )
                term = jnp.pad(term, ((0, 0), (1 + a, 1 - a), (0, 0)))
                seam = term if seam is None else seam + term
        sides.append(seam)
    pairs = zip(hex_terms[:5], hex_terms[5:] + time_terms)
    terms = jnp.stack([jnp.concatenate(pair, axis=-1) for pair in pairs])
    return spread, jnp.stack(sides).astype(jnp.bfloat16), terms


def seam_columns(block):
    return jnp.stack([block[..., block.shape[-1] - 1], block[..., 0]])


def shards(activations, upstream, hex_weight, time_weight, left_map, right_map):
    field = activations[:, 0]
    cotangent = upstream[:, 0]
    frames, tile_rows, channels, columns = field.shape
    chart, charts = lax.axis_index("diamond"), lax.axis_size("diamond")
    tile, tiles = lax.axis_index("tile"), lax.axis_size("tile")
    line, lines = lax.axis_index("tm"), lax.axis_size("tm")
    first_row = tile * tile_rows
    wide = tile_rows + 2
    strips = seam_columns(field).reshape(2, frames * tile_rows, channels)
    gathered, above, below, before, after = exchange_start(strips, field, cotangent)
    above = jnp.where(tile > 0, above, 0)
    below = jnp.where(tile < tiles - 1, below, 0)
    before = jnp.where(line > 0, before, 0)
    after = jnp.where(line < lines - 1, after, 0)

    def chart_rows(table, number):
        own = lax.dynamic_slice(table, (number, 0), (1, table.shape[1]))[0]
        return jnp.pad(own, (1, 1), constant_values=-1)

    every = jnp.arange(tiles * tile_rows)

    def ghost(strip, table):
        own = lax.dynamic_slice(chart_rows(table, chart), (first_row,), (wide,))
        pick = (own[:, None] == every[None, :]).astype(jnp.bfloat16)
        pick = pick.reshape(wide, tiles, tile_rows)
        strip = strip.reshape(tiles, frames, tile_rows, channels)
        return jnp.einsum("wtr,tfrc->fwc", pick, strip, preferred_element_type=jnp.float32).astype(
            jnp.bfloat16
        )

    ghost_left = ghost(gathered[:, 0], left_map)
    ghost_right = ghost(gathered[:, 1], right_map)
    rows = jnp.concatenate([above[:, None], field, below[:, None]], axis=1)
    padded = jnp.concatenate([ghost_left[..., None], rows, ghost_right[..., None]], axis=-1)
    framed = jnp.concatenate([before[None], cotangent, after[None]], axis=0)
    spread, seams, terms = local_math(
        padded, framed, hex_weight, time_weight, frames, tile_rows, channels, columns
    )
    strips = seams.reshape(2, frames * wide, channels)
    gathered, above, below, grad_hex, grad_time = exchange_end(
        strips, spread[:, 0].astype(jnp.bfloat16), spread[:, wide - 1].astype(jnp.bfloat16),
        terms.reshape(terms.shape[0], tiles, channels // tiles, 2 * channels),
    )
    total = cotangent.astype(jnp.float32) + spread[:, 1 : tile_rows + 1]
    above = jnp.where(tile > 0, above, 0).astype(jnp.float32)
    below = jnp.where(tile < tiles - 1, below, 0).astype(jnp.float32)
    total = total + jnp.pad(above[:, None], ((0, 0), (0, tile_rows - 1), (0, 0), (0, 0)))
    total = total + jnp.pad(below[:, None], ((0, 0), (tile_rows - 1, 0), (0, 0), (0, 0)))
    own_rows = first_row + jnp.arange(tile_rows)

    def landing(strip, table, number):
        target = chart_rows(table, number)
        inner = target[1:-1].reshape(tiles, tile_rows)
        prior = target[:-2].reshape(tiles, tile_rows)[:, :1]
        later = target[2:].reshape(tiles, tile_rows)[:, -1:]
        target = jnp.concatenate([prior, inner, later], axis=1)
        pick = (own_rows[:, None, None] == target[None]).astype(jnp.bfloat16)
        strip = strip.reshape(tiles, frames, wide, channels)
        return jnp.einsum("rtw,tfwc->frc", pick, strip, preferred_element_type=jnp.float32)

    into_first = landing(gathered[:, 0], right_map, lax.rem(chart + charts - 1, charts))
    into_last = landing(gathered[:, 1], left_map, lax.rem(chart + 1, charts))
    column = jnp.arange(columns)
    total = total + jnp.where(column == 0, into_first[..., None], 0.0)
    total = total + jnp.where(column == columns - 1, into_last[..., None], 0.0)
    return total.astype(jnp.bfloat16)[:, None], grad_hex, grad_time


def solution(mesh):
    whole = P("tm", "diamond", "tile", None, None)
    return jax.shard_map(
        shards,
        mesh=mesh,
        in_specs=(whole, whole, P(), P(), P(), P()),
        out_specs=(whole, P(), P()),
        check_vma=False,
    )
```

```python
import jax
import jax.numpy as jnp
from jax import lax
from jax.experimental import pallas as pl
from jax.experimental.pallas import tpu as pltpu
from jax.sharding import PartitionSpec as P

OFFSETS = ((0, 0), (0, 1), (0, -1), (1, 0), (-1, 0), (1, -1), (-1, 1))
ANY = pl.BlockSpec(memory_space=pl.ANY)
VMEM = pl.BlockSpec(memory_space=pltpu.VMEM)


def remote(src, dst, send_sem, recv_sem, device_id):
    return pltpu.make_async_remote_copy(
        src_ref=src,
        dst_ref=dst,
        send_sem=send_sem,
        recv_sem=recv_sem,
        device_id=device_id,
        device_id_type=pl.DeviceIdType.MESH,
    )


def meet(whole_tile, whole_group):
    me, tiles = lax.axis_index("tile"), lax.axis_size("tile")
    chart, charts = lax.axis_index("diamond"), lax.axis_size("diamond")
    line, lines = lax.axis_index("tm"), lax.axis_size("tm")
    mine, size = line * charts + chart, lines * charts
    partners = [
        {"diamond": lax.rem(chart + turn, charts), "tile": lax.rem(me + step, tiles)}
        for turn in sorted({1, charts - 1})
        for step in range(tiles)
    ]
    steps = range(1, tiles) if whole_tile else sorted({1, tiles - 1})
    partners += [{"tile": lax.rem(me + step, tiles)} for step in steps]
    if whole_group:
        others = [lax.rem(mine + step, size) for step in range(1, size)]
        partners += [{"tm": one // charts, "diamond": lax.rem(one, charts)} for one in others]
    else:
        partners += [{"tm": lax.rem(line + step, lines)} for step in sorted({1, lines - 1})]
    barrier = pltpu.get_barrier_semaphore()
    for partner in partners:
        pl.semaphore_signal(
            barrier, inc=1, device_id=partner, device_id_type=pl.DeviceIdType.MESH
        )
    pl.semaphore_wait(barrier, len(partners))


def line_copies(axis, to_next, at_next, to_prev, at_prev, send, recv):
    me, size = lax.axis_index(axis), lax.axis_size(axis)
    up = remote(to_next, at_next, send.at[0], recv.at[0], {axis: lax.rem(me + 1, size)})
    down = remote(to_prev, at_prev, send.at[1], recv.at[1], {axis: lax.rem(me + size - 1, size)})

    def start():
        pl.when(me < size - 1)(up.start)
        pl.when(me > 0)(down.start)

    def wait():
        pl.when(me < size - 1)(up.wait_send)
        pl.when(me > 0)(down.wait_send)
        pl.when(me > 0)(up.wait_recv)
        pl.when(me < size - 1)(down.wait_recv)

    return start, wait


def seam_copies(strips, gathered, send, recv):
    me, tiles = lax.axis_index("tile"), lax.axis_size("tile")
    chart, charts = lax.axis_index("diamond"), lax.axis_size("diamond")
    sides = (lax.rem(chart + 1, charts), lax.rem(chart + charts - 1, charts))
    parts = (slice(0, 2),) if charts == 2 else (slice(0, 1), slice(1, 2))

    def copy(part, step, source, target):
        return remote(
            strips.at[parts[part]],
            gathered.at[source, parts[part]],
            send.at[part, step],
            recv.at[part, source],
            {"diamond": sides[part], "tile": target},
        )

    copies = [
        copy(part, step, me, lax.rem(me + step, tiles))
        for step in range(tiles)
        for part in range(len(parts))
    ]

    def start():
        for one in copies:
            one.start()

    def wait():
        for one in copies:
            one.wait_send()
        for part in range(len(parts)):
            for number in range(tiles):
                copy(part, 0, number, me).wait_recv()

    return start, wait


def first_exchange(
    strips, field, cotangent, gathered, above, below, before, after,
    seam_send, seam_recv, row_send, row_recv, frame_send, frame_recv,
):
    meet(False, False)
    rows, frames = field.shape[1], field.shape[0]
    parts = (
        seam_copies(strips, gathered, seam_send, seam_recv),
        line_copies("tile", field.at[:, rows - 1], above, field.at[:, 0], below, row_send, row_recv),
        line_copies(
            "tm", cotangent.at[frames - 1], before, cotangent.at[0], after, frame_send, frame_recv
        ),
    )
    for start, _ in parts:
        start()
    for _, wait in parts:
        wait()


def last_exchange(
    strips, up_row, down_row, terms, gathered, above, below, grad_hex, grad_time,
    seam_send, seam_recv, row_send, row_recv, sums,
    scattered, scatter_send, scatter_recv, group, group_send, group_recv, out_send, out_recv,
):
    meet(True, True)
    me, tiles = lax.axis_index("tile"), lax.axis_size("tile")
    charts, lines = lax.axis_size("diamond"), lax.axis_size("tm")
    mine = lax.axis_index("tm") * charts + lax.axis_index("diamond")
    size = lines * charts

    def tile_copy(src, dst, send, recv, step):
        return remote(src, dst, send.at[step], recv, {"tile": lax.rem(me + step, tiles)})

    first = [
        tile_copy(
            terms.at[:, lax.rem(me + step, tiles)], scattered.at[me], scatter_send,
            scatter_recv.at[me], step,
        )
        for step in range(1, tiles)
    ]
    for copy in first:
        copy.start()
    parts = (
        seam_copies(strips, gathered, seam_send, seam_recv),
        line_copies("tile", down_row, above, up_row, below, row_send, row_recv),
    )
    for start, _ in parts:
        start()
    total = terms[:, me]
    for step in range(1, tiles):
        other = lax.rem(me + step, tiles)
        tile_copy(
            terms.at[:, other], scattered.at[other], scatter_send, scatter_recv.at[other], step
        ).wait_recv()
        total = total + scattered[other]
    group[mine] = total
    second = []
    for step in range(1, size):
        other = lax.rem(mine + step, size)
        target = {"tm": other // charts, "diamond": lax.rem(other, charts)}
        copy = remote(
            group.at[mine], group.at[mine], group_send.at[step], group_recv.at[mine], target
        )
        copy.start()
        second.append(copy)
    for step in range(1, size):
        other = lax.rem(mine + step, size)
        target = {"tm": other // charts, "diamond": lax.rem(other, charts)}
        remote(
            group.at[other], group.at[other], group_send.at[step], group_recv.at[other], target
        ).wait_recv()
    total = group[0]
    for number in range(1, size):
        total = total + group[number]
    sums[me] = total
    third = [
        tile_copy(sums.at[me], sums.at[me], out_send, out_recv.at[me], step)
        for step in range(1, tiles)
    ]
    for copy in third:
        copy.start()
    for step in range(1, tiles):
        other = lax.rem(me + step, tiles)
        tile_copy(sums.at[other], sums.at[other], out_send, out_recv.at[other], step).wait_recv()
    channels = grad_hex.shape[1]
    pairs, _, span, _ = terms.shape
    taps = grad_hex.shape[0]
    for number in range(tiles):
        chunk = sums[number]
        rows = pl.ds(number * span, span)
        grad_hex[:pairs, rows] = chunk[..., :channels]
        grad_hex[pairs:, rows] = chunk[: taps - pairs, :, channels:]
        grad_time[:, rows] = chunk[taps - pairs :, :, channels:]
    for copy in first + second + third:
        copy.wait_send()
    for _, wait in parts:
        wait()


def exchange_start(strips, field, cotangent):
    frames, rows, channels, columns = field.shape
    tiles = lax.axis_size("tile")
    dma = pltpu.SemaphoreType.DMA
    kind = field.dtype
    line = jax.ShapeDtypeStruct((frames, channels, columns), kind)
    frame = jax.ShapeDtypeStruct((rows, channels, columns), kind)
    return pl.pallas_call(
        first_exchange,
        out_shape=(
            jax.ShapeDtypeStruct((tiles,) + strips.shape, kind), line, line, frame, frame,
        ),
        in_specs=[VMEM, ANY, ANY],
        out_specs=(VMEM,) * 5,
        scratch_shapes=[
            dma((2, tiles)), dma((2, tiles)), dma((2,)), dma((2,)), dma((2,)), dma((2,)),
        ],
        compiler_params=pltpu.CompilerParams(collective_id=0, has_side_effects=True),
        name="first_exchange",
    )(strips, field, cotangent)


def exchange_end(strips, up_row, down_row, terms):
    tiles = lax.axis_size("tile")
    size = lax.axis_size("tm") * lax.axis_size("diamond")
    dma = pltpu.SemaphoreType.DMA
    line = jax.ShapeDtypeStruct(up_row.shape, up_row.dtype)
    chunk = terms.shape[:1] + terms.shape[2:]
    channels = up_row.shape[1]
    return pl.pallas_call(
        last_exchange,
        out_shape=(
            jax.ShapeDtypeStruct((tiles,) + strips.shape, strips.dtype), line, line,
            jax.ShapeDtypeStruct((7, channels, channels), terms.dtype),
            jax.ShapeDtypeStruct((3, channels, channels), terms.dtype),
        ),
        in_specs=[VMEM] * 4,
        out_specs=(VMEM,) * 5,
        scratch_shapes=[
            dma((2, tiles)), dma((2, tiles)), dma((2,)), dma((2,)),
            pltpu.VMEM((tiles,) + chunk, terms.dtype),
            pltpu.VMEM((tiles,) + chunk, terms.dtype), dma((tiles,)), dma((tiles,)),
            pltpu.VMEM((size,) + chunk, terms.dtype), dma((size,)), dma((size,)),
            dma((tiles,)), dma((tiles,)),
        ],
        compiler_params=pltpu.CompilerParams(collective_id=1, has_side_effects=True),
        name="last_exchange",
    )(strips, up_row, down_row, terms)


def silu_slope(hidden):
    sigmoid = jax.nn.sigmoid(hidden)
    return sigmoid * (1.0 + hidden * (1.0 - sigmoid))


def local_math(padded, framed, hex_weight, time_weight, frames, tile_rows, channels, columns):
    hidden = jnp.zeros((frames, tile_rows, channels, columns), jnp.float32)
    windows = [
        padded[:, 1 + a : 1 + a + tile_rows, :, 1 + b : 1 + b + columns] for a, b in OFFSETS
    ]
    for number in range(7):
        hidden = hidden + jnp.einsum(
            "frcx,cd->frdx", windows[number], hex_weight[number],
            preferred_element_type=jnp.float32,
        )
    active = jax.nn.silu(hidden).astype(jnp.bfloat16)
    grad_act = jnp.zeros((frames, tile_rows, channels, columns), jnp.float32)
    time_terms = []
    for number in range(3):
        shifted = framed[2 - number : 2 - number + frames]
        grad_act = grad_act + jnp.einsum(
            "frdx,cd->frcx", shifted, time_weight[number], preferred_element_type=jnp.float32
        )
        time_terms.append(
            jnp.einsum("frcx,frdx->cd", active, shifted, preferred_element_type=jnp.float32)
        )
    grad_wide = (grad_act * silu_slope(hidden)).astype(jnp.bfloat16)
    hex_terms = [
        jnp.einsum("frcx,frdx->cd", window, grad_wide, preferred_element_type=jnp.float32)
        for window in windows
    ]
    spread = None
    for number, (a, b) in enumerate(OFFSETS):
        term = jnp.einsum(
            "frdx,cd->frcx", grad_wide, hex_weight[number], preferred_element_type=jnp.float32
        )
        if b == 1:
            term = jnp.pad(term[..., :-1], ((0, 0), (0, 0), (0, 0), (1, 0)))
        if b == -1:
            term = jnp.pad(term[..., 1:], ((0, 0), (0, 0), (0, 0), (0, 1)))
        term = jnp.pad(term, ((0, 0), (1 + a, 1 - a), (0, 0), (0, 0)))
        spread = term if spread is None else spread + term
    seams = seam_columns(grad_wide)
    sides = []
    for side, b in ((0, 1), (1, -1)):
        seam = None
        for number, (a, _) in enumerate(OFFSETS):
            if OFFSETS[number][1] == b:
                term = jnp.einsum(
                    "frd,cd->frc", seams[side], hex_weight[number],
                    preferred_element_type=jnp.float32,
                )
                term = jnp.pad(term, ((0, 0), (1 + a, 1 - a), (0, 0)))
                seam = term if seam is None else seam + term
        sides.append(seam)
    pairs = zip(hex_terms[:5], hex_terms[5:] + time_terms)
    terms = jnp.stack([jnp.concatenate(pair, axis=-1) for pair in pairs])
    return spread, jnp.stack(sides).astype(jnp.bfloat16), terms


def seam_columns(block):
    return jnp.stack([block[..., block.shape[-1] - 1], block[..., 0]])


def shards(activations, upstream, hex_weight, time_weight, left_map, right_map):
    field = activations[:, 0]
    cotangent = upstream[:, 0]
    frames, tile_rows, channels, columns = field.shape
    chart, charts = lax.axis_index("diamond"), lax.axis_size("diamond")
    tile, tiles = lax.axis_index("tile"), lax.axis_size("tile")
    line, lines = lax.axis_index("tm"), lax.axis_size("tm")
    first_row = tile * tile_rows
    wide = tile_rows + 2
    strips = seam_columns(field).reshape(2, frames * tile_rows, channels)
    gathered, above, below, before, after = exchange_start(strips, field, cotangent)
    above = jnp.where(tile > 0, above, 0)
    below = jnp.where(tile < tiles - 1, below, 0)
    before = jnp.where(line > 0, before, 0)
    after = jnp.where(line < lines - 1, after, 0)

    def chart_rows(table, number):
        own = lax.dynamic_slice(table, (number, 0), (1, table.shape[1]))[0]
        return jnp.pad(own, (1, 1), constant_values=-1)

    every = jnp.arange(tiles * tile_rows)

    def ghost(strip, table):
        own = lax.dynamic_slice(chart_rows(table, chart), (first_row,), (wide,))
        pick = (own[:, None] == every[None, :]).astype(jnp.bfloat16)
        pick = pick.reshape(wide, tiles, tile_rows)
        strip = strip.reshape(tiles, frames, tile_rows, channels)
        return jnp.einsum("wtr,tfrc->fwc", pick, strip, preferred_element_type=jnp.float32).astype(
            jnp.bfloat16
        )

    ghost_left = ghost(gathered[:, 0], left_map)
    ghost_right = ghost(gathered[:, 1], right_map)
    rows = jnp.concatenate([above[:, None], field, below[:, None]], axis=1)
    padded = jnp.concatenate([ghost_left[..., None], rows, ghost_right[..., None]], axis=-1)
    framed = jnp.concatenate([before[None], cotangent, after[None]], axis=0)
    spread, seams, terms = local_math(
        padded, framed, hex_weight, time_weight, frames, tile_rows, channels, columns
    )
    strips = seams.reshape(2, frames * wide, channels)
    gathered, above, below, grad_hex, grad_time = exchange_end(
        strips, spread[:, 0].astype(jnp.bfloat16), spread[:, wide - 1].astype(jnp.bfloat16),
        terms.reshape(terms.shape[0], tiles, channels // tiles, 2 * channels),
    )
    total = cotangent.astype(jnp.float32) + spread[:, 1 : tile_rows + 1]
    above = jnp.where(tile > 0, above, 0).astype(jnp.float32)
    below = jnp.where(tile < tiles - 1, below, 0).astype(jnp.float32)
    total = total + jnp.pad(above[:, None], ((0, 0), (0, tile_rows - 1), (0, 0), (0, 0)))
    total = total + jnp.pad(below[:, None], ((0, 0), (tile_rows - 1, 0), (0, 0), (0, 0)))
    own_rows = first_row + jnp.arange(tile_rows)

    def landing(strip, table, number):
        target = chart_rows(table, number)
        inner = target[1:-1].reshape(tiles, tile_rows)
        prior = target[:-2].reshape(tiles, tile_rows)[:, :1]
        later = target[2:].reshape(tiles, tile_rows)[:, -1:]
        target = jnp.concatenate([prior, inner, later], axis=1)
        pick = (own_rows[:, None, None] == target[None]).astype(jnp.bfloat16)
        strip = strip.reshape(tiles, frames, wide, channels)
        return jnp.einsum("rtw,tfwc->frc", pick, strip, preferred_element_type=jnp.float32)

    into_first = landing(gathered[:, 0], right_map, lax.rem(chart + charts - 1, charts))
    into_last = landing(gathered[:, 1], left_map, lax.rem(chart + 1, charts))
    column = jnp.arange(columns)
    total = total + jnp.where(column == 0, into_first[..., None], 0.0)
    total = total + jnp.where(column == columns - 1, into_last[..., None], 0.0)
    return total.astype(jnp.bfloat16)[:, None], grad_hex, grad_time


def solution(mesh):
    whole = P("tm", "diamond", "tile", None, None)
    return jax.shard_map(
        shards,
        mesh=mesh,
        in_specs=(whole, whole, P(), P(), P(), P()),
        out_specs=(whole, P(), P()),
        check_vma=False,
    )
```

```python
import jax
import jax.numpy as jnp
from jax import lax
from jax.experimental import pallas as pl
from jax.experimental.pallas import tpu as pltpu
from jax.sharding import PartitionSpec as P

OFFSETS = ((0, 0), (0, 1), (0, -1), (1, 0), (-1, 0), (1, -1), (-1, 1))
ANY = pl.BlockSpec(memory_space=pl.ANY)
VMEM = pl.BlockSpec(memory_space=pltpu.VMEM)


def remote(src, dst, send_sem, recv_sem, device_id):
    return pltpu.make_async_remote_copy(
        src_ref=src,
        dst_ref=dst,
        send_sem=send_sem,
        recv_sem=recv_sem,
        device_id=device_id,
        device_id_type=pl.DeviceIdType.MESH,
    )


def meet(whole_tile, whole_group):
    me, tiles = lax.axis_index("tile"), lax.axis_size("tile")
    chart, charts = lax.axis_index("diamond"), lax.axis_size("diamond")
    line, lines = lax.axis_index("tm"), lax.axis_size("tm")
    mine, size = line * charts + chart, lines * charts
    partners = [
        {"diamond": lax.rem(chart + turn, charts), "tile": lax.rem(me + step, tiles)}
        for turn in sorted({1, charts - 1})
        for step in range(tiles)
    ]
    steps = range(1, tiles) if whole_tile else sorted({1, tiles - 1})
    partners += [{"tile": lax.rem(me + step, tiles)} for step in steps]
    if whole_group:
        others = [lax.rem(mine + step, size) for step in range(1, size)]
        partners += [{"tm": one // charts, "diamond": lax.rem(one, charts)} for one in others]
    else:
        partners += [{"tm": lax.rem(line + step, lines)} for step in sorted({1, lines - 1})]
    barrier = pltpu.get_barrier_semaphore()
    for partner in partners:
        pl.semaphore_signal(
            barrier, inc=1, device_id=partner, device_id_type=pl.DeviceIdType.MESH
        )
    pl.semaphore_wait(barrier, len(partners))


def line_copies(axis, to_next, at_next, to_prev, at_prev, send, recv):
    me, size = lax.axis_index(axis), lax.axis_size(axis)
    up = remote(to_next, at_next, send.at[0], recv.at[0], {axis: lax.rem(me + 1, size)})
    down = remote(to_prev, at_prev, send.at[1], recv.at[1], {axis: lax.rem(me + size - 1, size)})

    def start():
        pl.when(me < size - 1)(up.start)
        pl.when(me > 0)(down.start)

    def wait():
        pl.when(me < size - 1)(up.wait_send)
        pl.when(me > 0)(down.wait_send)
        pl.when(me > 0)(up.wait_recv)
        pl.when(me < size - 1)(down.wait_recv)

    return start, wait


def seam_copies(strips, gathered, send, recv):
    me, tiles = lax.axis_index("tile"), lax.axis_size("tile")
    chart, charts = lax.axis_index("diamond"), lax.axis_size("diamond")
    sides = (lax.rem(chart + 1, charts), lax.rem(chart + charts - 1, charts))
    parts = (slice(0, 2),) if charts == 2 else (slice(0, 1), slice(1, 2))

    def copy(part, step, source, target):
        return remote(
            strips.at[parts[part]],
            gathered.at[source, parts[part]],
            send.at[part, step],
            recv.at[part, source],
            {"diamond": sides[part], "tile": target},
        )

    copies = [
        copy(part, step, me, lax.rem(me + step, tiles))
        for step in range(tiles)
        for part in range(len(parts))
    ]

    def start():
        for one in copies:
            one.start()

    def wait():
        for one in copies:
            one.wait_send()
        for part in range(len(parts)):
            for number in range(tiles):
                copy(part, 0, number, me).wait_recv()

    return start, wait


def first_exchange(
    strips, field, cotangent, gathered, above, below, before, after,
    seam_send, seam_recv, row_send, row_recv, frame_send, frame_recv,
):
    meet(False, False)
    rows, frames = field.shape[1], field.shape[0]
    parts = (
        seam_copies(strips, gathered, seam_send, seam_recv),
        line_copies("tile", field.at[:, rows - 1], above, field.at[:, 0], below, row_send, row_recv),
        line_copies(
            "tm", cotangent.at[frames - 1], before, cotangent.at[0], after, frame_send, frame_recv
        ),
    )
    for start, _ in parts:
        start()
    for _, wait in parts:
        wait()


def last_exchange(
    strips, up_row, down_row, terms, gathered, above, below, grad_hex, grad_time,
    seam_send, seam_recv, row_send, row_recv, sums,
    scattered, scatter_send, scatter_recv, group, group_send, group_recv, out_send, out_recv,
):
    meet(True, True)
    me, tiles = lax.axis_index("tile"), lax.axis_size("tile")
    charts, lines = lax.axis_size("diamond"), lax.axis_size("tm")
    mine = lax.axis_index("tm") * charts + lax.axis_index("diamond")
    size = lines * charts

    def tile_copy(src, dst, send, recv, step):
        return remote(src, dst, send.at[step], recv, {"tile": lax.rem(me + step, tiles)})

    first = [
        tile_copy(
            terms.at[:, lax.rem(me + step, tiles)], scattered.at[me], scatter_send,
            scatter_recv.at[me], step,
        )
        for step in range(1, tiles)
    ]
    for copy in first:
        copy.start()
    parts = (
        seam_copies(strips, gathered, seam_send, seam_recv),
        line_copies("tile", down_row, above, up_row, below, row_send, row_recv),
    )
    for start, _ in parts:
        start()
    total = terms[:, me]
    for step in range(1, tiles):
        other = lax.rem(me + step, tiles)
        tile_copy(
            terms.at[:, other], scattered.at[other], scatter_send, scatter_recv.at[other], step
        ).wait_recv()
        total = total + scattered[other]
    group[mine] = total
    second = []
    for step in range(1, size):
        other = lax.rem(mine + step, size)
        target = {"tm": other // charts, "diamond": lax.rem(other, charts)}
        copy = remote(
            group.at[mine], group.at[mine], group_send.at[step], group_recv.at[mine], target
        )
        copy.start()
        second.append(copy)
    for step in range(1, size):
        other = lax.rem(mine + step, size)
        target = {"tm": other // charts, "diamond": lax.rem(other, charts)}
        remote(
            group.at[other], group.at[other], group_send.at[step], group_recv.at[other], target
        ).wait_recv()
    total = group[0]
    for number in range(1, size):
        total = total + group[number]
    sums[me] = total
    third = [
        tile_copy(sums.at[me], sums.at[me], out_send, out_recv.at[me], step)
        for step in range(1, tiles)
    ]
    for copy in third:
        copy.start()
    for step in range(1, tiles):
        other = lax.rem(me + step, tiles)
        tile_copy(sums.at[other], sums.at[other], out_send, out_recv.at[other], step).wait_recv()
    channels = grad_hex.shape[1]
    pairs, _, span, _ = terms.shape
    taps = grad_hex.shape[0]
    for number in range(tiles):
        chunk = sums[number]
        rows = pl.ds(number * span, span)
        grad_hex[:pairs, rows] = chunk[..., :channels]
        grad_hex[pairs:, rows] = chunk[: taps - pairs, :, channels:]
        grad_time[:, rows] = chunk[taps - pairs :, :, channels:]
    for copy in first + second + third:
        copy.wait_send()
    for _, wait in parts:
        wait()


def exchange_start(strips, field, cotangent):
    frames, rows, channels, columns = field.shape
    tiles = lax.axis_size("tile")
    dma = pltpu.SemaphoreType.DMA
    kind = field.dtype
    line = jax.ShapeDtypeStruct((frames, channels, columns), kind)
    frame = jax.ShapeDtypeStruct((rows, channels, columns), kind)
    return pl.pallas_call(
        first_exchange,
        out_shape=(
            jax.ShapeDtypeStruct((tiles,) + strips.shape, kind), line, line, frame, frame,
        ),
        in_specs=[ANY] * 3,
        out_specs=(ANY,) * 5,
        scratch_shapes=[
            dma((2, tiles)), dma((2, tiles)), dma((2,)), dma((2,)), dma((2,)), dma((2,)),
        ],
        compiler_params=pltpu.CompilerParams(collective_id=0, has_side_effects=True),
        name="first_exchange",
    )(strips, field, cotangent)


def exchange_end(strips, up_row, down_row, terms):
    tiles = lax.axis_size("tile")
    size = lax.axis_size("tm") * lax.axis_size("diamond")
    dma = pltpu.SemaphoreType.DMA
    line = jax.ShapeDtypeStruct(up_row.shape, up_row.dtype)
    chunk = terms.shape[:1] + terms.shape[2:]
    channels = up_row.shape[1]
    return pl.pallas_call(
        last_exchange,
        out_shape=(
            jax.ShapeDtypeStruct((tiles,) + strips.shape, strips.dtype), line, line,
            jax.ShapeDtypeStruct((7, channels, channels), terms.dtype),
            jax.ShapeDtypeStruct((3, channels, channels), terms.dtype),
        ),
        in_specs=[ANY, ANY, ANY, VMEM],
        out_specs=(ANY, ANY, ANY, VMEM, VMEM),
        scratch_shapes=[
            dma((2, tiles)), dma((2, tiles)), dma((2,)), dma((2,)),
            pltpu.VMEM((tiles,) + chunk, terms.dtype),
            pltpu.VMEM((tiles,) + chunk, terms.dtype), dma((tiles,)), dma((tiles,)),
            pltpu.VMEM((size,) + chunk, terms.dtype), dma((size,)), dma((size,)),
            dma((tiles,)), dma((tiles,)),
        ],
        compiler_params=pltpu.CompilerParams(collective_id=1, has_side_effects=True),
        name="last_exchange",
    )(strips, up_row, down_row, terms)


def silu_slope(hidden):
    sigmoid = jax.nn.sigmoid(hidden)
    return sigmoid * (1.0 + hidden * (1.0 - sigmoid))


def local_math(padded, framed, hex_weight, time_weight, frames, tile_rows, channels, columns):
    hidden = jnp.zeros((frames, tile_rows, channels, columns), jnp.float32)
    windows = [
        padded[:, 1 + a : 1 + a + tile_rows, :, 1 + b : 1 + b + columns] for a, b in OFFSETS
    ]
    for number in range(7):
        hidden = hidden + jnp.einsum(
            "frcx,cd->frdx", windows[number], hex_weight[number],
            preferred_element_type=jnp.float32,
        )
    active = jax.nn.silu(hidden).astype(jnp.bfloat16)
    grad_act = jnp.zeros((frames, tile_rows, channels, columns), jnp.float32)
    time_terms = []
    for number in range(3):
        shifted = framed[2 - number : 2 - number + frames]
        grad_act = grad_act + jnp.einsum(
            "frdx,cd->frcx", shifted, time_weight[number], preferred_element_type=jnp.float32
        )
        time_terms.append(
            jnp.einsum("frcx,frdx->cd", active, shifted, preferred_element_type=jnp.float32)
        )
    grad_wide = (grad_act * silu_slope(hidden)).astype(jnp.bfloat16)
    hex_terms = [
        jnp.einsum("frcx,frdx->cd", window, grad_wide, preferred_element_type=jnp.float32)
        for window in windows
    ]
    spread = up_row = down_row = None
    for number, (a, b) in enumerate(OFFSETS):
        term = jnp.einsum(
            "frdx,cd->frcx", grad_wide, hex_weight[number], preferred_element_type=jnp.float32
        )
        if b == 1:
            term = jnp.pad(term[..., :-1], ((0, 0), (0, 0), (0, 0), (1, 0)))
        if b == -1:
            term = jnp.pad(term[..., 1:], ((0, 0), (0, 0), (0, 0), (0, 1)))
        if a == 1:
            down_row = term[:, -1] if down_row is None else down_row + term[:, -1]
            term = jnp.pad(term[:, :-1], ((0, 0), (1, 0), (0, 0), (0, 0)))
        if a == -1:
            up_row = term[:, 0] if up_row is None else up_row + term[:, 0]
            term = jnp.pad(term[:, 1:], ((0, 0), (0, 1), (0, 0), (0, 0)))
        spread = term if spread is None else spread + term
    edges = up_row.astype(jnp.bfloat16), down_row.astype(jnp.bfloat16)
    seams = seam_columns(grad_wide)
    sides = []
    for side, b in ((0, 1), (1, -1)):
        seam = None
        for number, (a, _) in enumerate(OFFSETS):
            if OFFSETS[number][1] == b:
                term = jnp.einsum(
                    "frd,cd->frc", seams[side], hex_weight[number],
                    preferred_element_type=jnp.float32,
                )
                term = jnp.pad(term, ((0, 0), (1 + a, 1 - a), (0, 0)))
                seam = term if seam is None else seam + term
        sides.append(seam)
    pairs = zip(hex_terms[:5], hex_terms[5:] + time_terms)
    terms = jnp.stack([jnp.concatenate(pair, axis=-1) for pair in pairs])
    return spread, edges, jnp.stack(sides).astype(jnp.bfloat16), terms


def seam_columns(block):
    return jnp.stack([block[..., block.shape[-1] - 1], block[..., 0]])


def shards(activations, upstream, hex_weight, time_weight, left_map, right_map):
    field = activations[:, 0]
    cotangent = upstream[:, 0]
    frames, tile_rows, channels, columns = field.shape
    chart, charts = lax.axis_index("diamond"), lax.axis_size("diamond")
    tile, tiles = lax.axis_index("tile"), lax.axis_size("tile")
    line, lines = lax.axis_index("tm"), lax.axis_size("tm")
    first_row = tile * tile_rows
    wide = tile_rows + 2
    strips = seam_columns(field).reshape(2, frames * tile_rows, channels)
    gathered, above, below, before, after = exchange_start(strips, field, cotangent)
    above = jnp.where(tile > 0, above, 0)
    below = jnp.where(tile < tiles - 1, below, 0)
    before = jnp.where(line > 0, before, 0)
    after = jnp.where(line < lines - 1, after, 0)

    def chart_rows(table, number):
        own = lax.dynamic_slice(table, (number, 0), (1, table.shape[1]))[0]
        return jnp.pad(own, (1, 1), constant_values=-1)

    every = jnp.arange(tiles * tile_rows)

    def ghost(strip, table):
        own = lax.dynamic_slice(chart_rows(table, chart), (first_row,), (wide,))
        pick = (own[:, None] == every[None, :]).astype(jnp.bfloat16)
        pick = pick.reshape(wide, tiles, tile_rows)
        strip = strip.reshape(tiles, frames, tile_rows, channels)
        return jnp.einsum("wtr,tfrc->fwc", pick, strip, preferred_element_type=jnp.float32).astype(
            jnp.bfloat16
        )

    ghost_left = ghost(gathered[:, 0], left_map)
    ghost_right = ghost(gathered[:, 1], right_map)
    rows = jnp.concatenate([above[:, None], field, below[:, None]], axis=1)
    padded = jnp.concatenate([ghost_left[..., None], rows, ghost_right[..., None]], axis=-1)
    framed = jnp.concatenate([before[None], cotangent, after[None]], axis=0)
    spread, edges, seams, terms = local_math(
        padded, framed, hex_weight, time_weight, frames, tile_rows, channels, columns
    )
    strips = seams.reshape(2, frames * wide, channels)
    gathered, above, below, grad_hex, grad_time = exchange_end(
        strips, *edges, terms.reshape(terms.shape[0], tiles, channels // tiles, 2 * channels)
    )
    row = jnp.arange(tile_rows)[:, None, None]
    total = cotangent.astype(jnp.float32) + spread
    total = total + jnp.where(
        (row == 0) & (tile > 0), above[:, None].astype(jnp.float32), 0.0
    )
    total = total + jnp.where(
        (row == tile_rows - 1) & (tile < tiles - 1), below[:, None].astype(jnp.float32), 0.0
    )
    own_rows = first_row + jnp.arange(tile_rows)

    def landing(strip, table, number):
        target = chart_rows(table, number)
        inner = target[1:-1].reshape(tiles, tile_rows)
        prior = target[:-2].reshape(tiles, tile_rows)[:, :1]
        later = target[2:].reshape(tiles, tile_rows)[:, -1:]
        target = jnp.concatenate([prior, inner, later], axis=1)
        pick = (own_rows[:, None, None] == target[None]).astype(jnp.bfloat16)
        strip = strip.reshape(tiles, frames, wide, channels)
        return jnp.einsum("rtw,tfwc->frc", pick, strip, preferred_element_type=jnp.float32)

    into_first = landing(gathered[:, 0], right_map, lax.rem(chart + charts - 1, charts))
    into_last = landing(gathered[:, 1], left_map, lax.rem(chart + 1, charts))
    column = jnp.arange(columns)
    total = total + jnp.where(column == 0, into_first[..., None], 0.0)
    total = total + jnp.where(column == columns - 1, into_last[..., None], 0.0)
    return total.astype(jnp.bfloat16)[:, None], grad_hex, grad_time


def solution(mesh):
    whole = P("tm", "diamond", "tile", None, None)
    return jax.shard_map(
        shards,
        mesh=mesh,
        in_specs=(whole, whole, P(), P(), P(), P()),
        out_specs=(whole, P(), P()),
        check_vma=False,
    )
```
